256 devices in a mesh: sub: 64 (over z, y, core), rhs: 4 (over x).
Axes of the slice: x: 4, y: 4, z: 8, core: 2. Of those that a mesh axis runs over, the one named last changes fastest.
Arguments:
- stiffness: float32 [3072, 4, 9216], P('sub'), may hold values from -1 to 2, as said below
- precond: float32 [3072, 9216], P('sub'), may hold values from -0.625 to 0.625
- rhs_vec: float32 [8, 294912], P('rhs', 'sub'), may hold values from -50 to 50
- cotangent: float32 [8, 294912], P('rhs', 'sub'), may hold values from -6 to 6
- col_index: int32 [3072, 4], P('sub'), may hold values from 0 to 59, as said below
- send_rows: int32 [64, 12], P('sub'), may hold values from 0 to 47, as said below
- counts: int32 [64], P('sub'), may hold values from 12 to 48, as said below
Outputs:
- solution: float32 [8, 294912], P('rhs', 'sub')
- grad_precond: float32 [3072, 9216], P('sub')
The draws below stay inside these ranges and needn't reach their ends.
Inputs may be any that keep to these rules, and one draw needn't show every extreme that they name: `counts`: at least one subdomain has 48 live block rows. `send_rows`: for subdomain s, entries 0 to 5 are distinct live rows below counts[s] // 2 in increasing order, the first of them 0; entries 6 to 11 are distinct live rows from counts[s] // 2 on in increasing order, the last of them counts[s] - 1. Interface row j of the first group of subdomain s is coupled with interface row j of the second group of subdomain s - 1. `col_index`: index 6 + n is block n of the subdomain; indices below 6 and from 54 on are the blocks received from the previous and the next subdomain. Slot 0 of row n is 6 + n. A slot other than slot 0 that names 6 + n holds a zero block; rows that are not live hold only slot 0's block. `stiffness`: the operator A is symmetric and positive definite.
All inputs are finite; a program needn't handle non-finite values.
Results may differ from the reference program's by a relative error of at most 0.0003.
Values sent between devices are 32-bit elements; how exact they have to be, the bound alone decides.
A program may use at most 128 MiB of HBM per device.

```python
import jax
import jax.numpy as jnp
from jax import lax

BS = 96
K = 4
NBLK = 48
IF = 6
ITERS = 4
RHS = 8
SUBS = 64
BLOCKS = 3072


def layout(key):
    raw_draw = jax.random.randint(jax.random.fold_in(key, 11), (SUBS,), 0, 64)
    cube_val = raw_draw * raw_draw * raw_draw // 4096
    live_rows = NBLK // 4 + (NBLK - NBLK // 4) * cube_val // 64
    heaviest = jax.random.randint(jax.random.fold_in(key, 12), (), 0, SUBS)
    live_rows = jnp.where(jnp.arange(SUBS) == heaviest, NBLK, live_rows).astype(jnp.int32)
    position = jnp.arange(NBLK)[None, :]
    half_mark = (live_rows // 2)[:, None]
    limit = (1 << 16) * NBLK
    scores_left = jax.random.randint(jax.random.fold_in(key, 13), (SUBS, NBLK), 0, 1 << 16) * NBLK + position
    scores_right = jax.random.randint(jax.random.fold_in(key, 14), (SUBS, NBLK), 0, 1 << 16) * NBLK + position
    left_keys = jnp.where(position < half_mark, scores_left, limit + position)
    left_keys = jnp.where(position == 0, -1, left_keys)
    right_ok = (position >= half_mark) & (position < live_rows[:, None])
    right_keys = jnp.where(right_ok, scores_right, limit + position)
    right_keys = jnp.where(position == live_rows[:, None] - 1, -1, right_keys)
    left_pick = jnp.sort(jnp.argsort(left_keys, axis=1)[:, :IF], axis=1)
    right_pick = jnp.sort(jnp.argsort(right_keys, axis=1)[:, :IF], axis=1)
    sending = jnp.concatenate([left_pick, right_pick], axis=1).astype(jnp.int32)
    return (live_rows, sending)


def draw_counts(key, part):
    return layout(key)[0]


def draw_send_rows(key, part):
    return layout(key)[1]


def draw_col_index(key, part):
    live_rows, sending = layout(key)
    row_index = jnp.arange(NBLK)[None, :]
    own_col = jnp.broadcast_to(IF + row_index, (SUBS, NBLK))
    lower_col = jnp.where((row_index >= 1) & (row_index < live_rows[:, None]), own_col - 1, own_col)
    upper_col = jnp.where(row_index + 1 < live_rows[:, None], own_col + 1, own_col)
    sub_ids = jnp.arange(SUBS)[:, None]
    outer_col = own_col.at[sub_ids, sending[:, :IF]].set(jnp.broadcast_to(jnp.arange(IF)[None, :], (SUBS, IF)))
    outer_col = outer_col.at[sub_ids, sending[:, IF:]].set(jnp.broadcast_to(IF + NBLK + jnp.arange(IF)[None, :], (SUBS, IF)))
    column_table = jnp.stack([own_col, lower_col, upper_col, outer_col], axis=2)
    return column_table.reshape(SUBS * NBLK, K).astype(jnp.int32)


def draw_stiffness(key, part):
    live_rows, sending = layout(key)
    entry_bound = 0.8 / (4 * BS - 1)
    centre_raw = jax.random.uniform(jax.random.fold_in(key, 21), (SUBS, NBLK, BS, BS), jnp.float32, -entry_bound, entry_bound)
    centre_raw = 0.5 * (centre_raw + jnp.swapaxes(centre_raw, -1, -2))
    identity = jnp.eye(BS, dtype=jnp.float32)
    diag_vals = jax.random.uniform(jax.random.fold_in(key, 22), (SUBS, NBLK, BS), jnp.float32, 1.0, 2.0)
    centre = centre_raw * (1.0 - identity) + identity * diag_vals[..., None]
    edge_blocks = jax.random.uniform(jax.random.fold_in(key, 23), (SUBS, NBLK, BS, BS), jnp.float32, -entry_bound, entry_bound)
    row_index = jnp.arange(NBLK)[None, :]
    edge_ok = (row_index + 1 < live_rows[:, None]).astype(jnp.float32)
    upper_blk = edge_blocks * edge_ok[..., None, None]
    flipped = jnp.swapaxes(upper_blk, -1, -2)
    lower_blk = jnp.concatenate([jnp.zeros_like(flipped[:, :1]), flipped[:, :-1]], axis=1)
    face_blocks = jax.random.uniform(jax.random.fold_in(key, 24), (SUBS, IF, BS, BS), jnp.float32, -entry_bound, entry_bound)
    has_left = (jnp.arange(SUBS) >= 1).astype(jnp.float32)
    left_blk = face_blocks * has_left[:, None, None, None]
    right_src = jnp.concatenate([face_blocks[1:], jnp.zeros_like(face_blocks[:1])], axis=0)
    right_blk = jnp.swapaxes(right_src, -1, -2)
    sub_ids = jnp.arange(SUBS)[:, None]
    outer_blk = jnp.zeros((SUBS, NBLK, BS, BS), jnp.float32)
    outer_blk = outer_blk.at[sub_ids, sending[:, :IF]].set(left_blk)
    outer_blk = outer_blk.at[sub_ids, sending[:, IF:]].set(right_blk)
    stacked = jnp.stack([centre, lower_blk, upper_blk, outer_blk], axis=2)
    return stacked.reshape(SUBS * NBLK, K, BS * BS)


def draw_rhs_vec(key, part):
    sub_pos = (jnp.arange(BLOCKS * BS) // (NBLK * BS)).astype(jnp.float32)
    spread = jax.random.uniform(jax.random.fold_in(key, 32), (RHS, BLOCKS), jnp.float32, jnp.log(0.5), jnp.log(2.0))
    block_scale = jnp.repeat(jnp.exp(spread), BS, axis=1)
    sub_ramp = 1.0 + 2.0 * sub_pos / max(SUBS - 1, 1)
    base_noise = jnp.clip(jax.random.normal(jax.random.fold_in(key, 31), (RHS, BLOCKS * BS), jnp.float32), -6.0, 6.0)
    return base_noise * sub_ramp[None, :] * block_scale


def level_of(rng, shape, split, smallest, top_value):
    def one(dim, blocks):
        draws = jax.random.uniform(jax.random.fold_in(jax.random.fold_in(rng, 6), dim), (blocks,), jnp.float32, smallest / len(split), top_value / len(split))
        return jnp.repeat(jnp.exp(draws), shape[dim] // blocks).reshape((-1,) + (1,) * (len(shape) - dim - 1))

    loudness = one(*split[0])
    for cut in split[1:]:
        loudness = loudness * one(*cut)
    return loudness


def normal_values(stream_key, extent, width, bound, cuts=(), kind=jnp.bfloat16):
    entries = width * jax.random.normal(stream_key, extent, jnp.float32)
    if cuts:
        entries = entries * level_of(stream_key, extent, cuts, -0.22, 0.18)
    return jnp.clip(entries, -bound, bound).astype(kind)


def setup_inputs(seed: int = 0) -> dict:
    key_of = jax.random.split(jax.random.key(seed), 8)
    return {
        "stiffness": draw_stiffness(jax.random.fold_in(key_of[7], 71), 0),
        "precond": normal_values(key_of[1], (BLOCKS, BS * BS), BS ** -0.5, 0.625, ((0, 64),), jnp.float32),
        "rhs_vec": draw_rhs_vec(jax.random.fold_in(key_of[7], 71), 0),
        "cotangent": normal_values(key_of[3], (RHS, BLOCKS * BS), 1.0, 6.0, ((0, 4), (1, 64)), jnp.float32),
        "col_index": draw_col_index(jax.random.fold_in(key_of[7], 71), 0),
        "send_rows": draw_send_rows(jax.random.fold_in(key_of[7], 71), 0),
        "counts": draw_counts(jax.random.fold_in(key_of[7], 71), 0),
    }


highest = lax.Precision.HIGHEST

def reference(stiffness, precond, rhs_vec, cotangent, col_index, send_rows, counts):
    sub_count = counts.shape[0]
    rhs_count = rhs_vec.shape[0]
    sub_ids = jnp.arange(sub_count)
    blocks = stiffness.reshape(sub_count, NBLK, K, BS, BS)
    columns = col_index.reshape(sub_count, NBLK * K)
    live_mask = (jnp.arange(NBLK)[None, :] < counts[:, None]).astype(rhs_vec.dtype)
    source = rhs_vec.reshape(rhs_count, sub_count, NBLK, BS) * live_mask[None, :, :, None]
    target = cotangent.reshape(rhs_count, sub_count, NBLK, BS)

    def apply_stiff(vector):
        outgoing = vector[:, sub_ids[:, None], send_rows]
        empty_rim = jnp.zeros_like(outgoing[:, :1, :IF])
        from_left = jnp.concatenate([empty_rim, outgoing[:, :-1, IF:]], axis=1)
        from_right = jnp.concatenate([outgoing[:, 1:, :IF], empty_rim], axis=1)
        extended = jnp.concatenate([from_left, vector, from_right], axis=2)
        gathered = extended[:, sub_ids[:, None], columns].reshape(rhs_count, sub_count, NBLK, K, BS)
        return jnp.einsum('snkab,rsnkb->rsna', blocks, gathered, precision=highest)

    def precond_apply(weights, vector):
        projected = jnp.einsum('snab,rsnb->rsna', weights, vector, precision=highest)
        return vector + jnp.einsum('snab,rsna->rsnb', weights, projected, precision=highest)

    def inner_sum(first_vec, second_vec):
        return lax.optimization_barrier(jnp.sum(first_vec * second_vec, axis=(1, 2, 3)))

    def widen(scalars):
        return scalars[:, None, None, None]

    def solve(flat_weights):
        weights = flat_weights.reshape(sub_count, NBLK, BS, BS)
        residual = source
        precon = precond_apply(weights, residual)
        direction = precon
        norm_now = inner_sum(residual, precon)
        solution = jnp.zeros_like(source)
        for iteration in range(ITERS):
            applied = apply_stiff(direction)
            step_len = norm_now / inner_sum(direction, applied)
            solution = solution + widen(step_len) * direction
            residual = residual - widen(step_len) * applied
            if iteration + 1 < ITERS:
                precon = precond_apply(weights, residual)
                norm_next = inner_sum(residual, precon)
                direction = precon + widen(norm_next / norm_now) * direction
                norm_now = norm_next
        return solution
    solution, pullback = jax.vjp(solve, precond)
    gradient, = pullback(target)
    return (solution.reshape(rhs_count, sub_count * NBLK * BS), gradient)
```

```python
import functools

import jax
import jax.numpy as jnp
from jax import lax
from jax.experimental import pallas as pl
from jax.experimental.pallas import tpu as pltpu
from jax.sharding import PartitionSpec as P

BS = 96
K = 4
NBLK = 48
IF = 6
ITERS = 4
LR = 2
LANES = 128
TILES = NBLK // 8
CHUNKS = BS * BS // LANES
GROUPS = CHUNKS // 3
VEC = LR * NBLK
ROWS = LR * BS * NBLK // LANES
PLANE = 8
UNROLL = 6
HALOS = 8
REDS = 6
EXT = 64
MESH = pl.DeviceIdType.MESH


def lane_iota():
    return lax.broadcasted_iota(jnp.int32, (8, LANES), 1)


def patterns(x, lane):
    far = pltpu.roll(x, 96, 1)
    mid = pltpu.roll(x, 64, 1)
    near = pltpu.roll(x, 32, 1)
    return (
        jnp.where(lane < 96, x, far),
        jnp.where(lane < 64, far, mid),
        jnp.where(lane < 32, mid, near),
    )


def row_parts(p, lane):
    zero = jnp.zeros_like(p[0])
    return (
        jnp.where(lane < 96, p[0], zero),
        jnp.where(lane < 64, p[1], jnp.where(lane >= 96, p[0], zero)),
        jnp.where(lane >= 64, p[1], jnp.where(lane < 32, p[2], zero)),
        jnp.where(lane >= 32, p[2], zero),
    )


def rows_to_chunks(r, lane):
    far = pltpu.roll(r[1], 96, 1)
    mid = pltpu.roll(r[2], 64, 1)
    return (
        jnp.where(lane < 96, r[0], far),
        jnp.where(lane < 64, far, mid),
        jnp.where(lane < 32, mid, pltpu.roll(r[3], 32, 1)),
    )


def chunks_to_rows(c, lane):
    zero = jnp.zeros_like(c[0])
    rows = (
        c[0],
        pltpu.roll(jnp.where(lane >= 96, c[0], c[1]), 32, 1),
        pltpu.roll(jnp.where(lane >= 64, c[1], c[2]), 64, 1),
        pltpu.roll(c[2], 96, 1),
    )
    return [jnp.where(lane < 96, r, zero) for r in rows]


def kernel(
    planes, nrhs,
    col_ref, send_ref, count_ref, rhs_ref, cot_ref, stiff_hbm, pre_hbm,
    sol_ref, grad_hbm,
    raw, blocks, weights, colx, ext, gat, nvec, hvec, tvec, tmv, utv, atv, yv, kv, xv,
    pbv, rbv, arbv,
    ph, qh, sh, zh, wh, rh, uh, scr, hsend, hrecv, rb1, rb2, fl, fr, gb, go,
    load_sem, out_sem, hs_sem, hr_sem, r1s, r1r, r2s, r2r, fs_sem, fr_sem,
):
    sub = lax.axis_index("sub")
    me = lax.axis_index("rhs")
    nsub = planes * PLANE
    plane = lax.div(sub, PLANE)
    spot = lax.rem(sub, PLANE)
    lane = lane_iota()

    def in_plane(d):
        return plane * PLANE + lax.rem(spot + d, PLANE)

    def across(d):
        return lax.rem(plane + d, planes) * PLANE + spot

    pre_copy = pltpu.make_async_copy(pre_hbm, weights, load_sem.at[TILES])
    pre_copy.start()
    stiff_copies = [
        pltpu.make_async_copy(stiff_hbm.at[t], raw.at[t], load_sem.at[t])
        for t in range(TILES)
    ]
    for copy in stiff_copies:
        copy.start()

    barrier = pltpu.get_barrier_semaphore()
    peers = 0
    for d in range(1, PLANE):
        pl.semaphore_signal(barrier, inc=1, device_id={"sub": in_plane(d)}, device_id_type=MESH)
        peers += 1
    for d in range(1, planes):
        pl.semaphore_signal(barrier, inc=1, device_id={"sub": across(d)}, device_id_type=MESH)
        peers += 1
    for d in range(1, nrhs):
        pl.semaphore_signal(barrier, inc=1, device_id={"rhs": lax.rem(me + d, nrhs)}, device_id_type=MESH)
        peers += 1
    before = lax.rem(sub + nsub - 1, nsub)
    after = lax.rem(sub + 1, nsub)
    for other in (before, after):
        pl.semaphore_signal(barrier, inc=1, device_id={"sub": other}, device_id_type=MESH)
        peers += 1

    for n in range(NBLK):
        for k in range(1, K):
            c = col_ref[n, k]
            colx[n * K + k] = jnp.where(
                c < IF, c + NBLK, jnp.where(c < IF + NBLK, c - IF, c + 8 - IF)
            )
    hsend[...] = jnp.zeros_like(hsend)
    for ref in (ph, qh, sh):
        ref[pl.ds(0, VEC), :] = jnp.zeros((VEC, LANES), jnp.float32)
    for ref in (yv, kv, xv, rbv, arbv):
        ref[...] = jnp.zeros_like(ref)

    lane12 = lax.broadcasted_iota(jnp.int32, (12, LANES), 1)
    row12 = lax.broadcasted_iota(jnp.int32, (12, LANES), 0)
    live = count_ref[0]
    for r in range(LR):
        chunks = [rhs_ref[pl.ds(2 * i + r, 12, stride=6), :] for i in range(3)]
        for j, row in enumerate(chunks_to_rows(chunks, lane12)):
            row = jnp.where(row12 * 4 + j < live, row, jnp.zeros_like(row))
            rh[pl.ds(r * NBLK + j, 12, stride=4), :] = row
        chunks = [cot_ref[pl.ds(2 * i + r, 12, stride=6), :] for i in range(3)]
        for j, row in enumerate(chunks_to_rows(chunks, lane12)):
            tvec[pl.ds(r * NBLK + j, 12, stride=4), :] = row

    def precondition(src, base, dst, dst_base, slot):
        full = slot is not None

        def tile(t, _):
            x = [src[pl.ds(pl.multiple_of(base + r * NBLK + 8 * t, 8), 8), :] for r in range(LR)]
            pat = [patterns(v, lane) for v in x]
            zero = jnp.zeros((8, LANES), jnp.float32)

            def step(s, carry):
                proj, acc = carry
                proj, acc = list(proj), [list(a) for a in acc]
                for q in range(UNROLL):
                    g = s * UNROLL + q
                    w = [weights[t, 3 * g + i] for i in range(3)]
                    for r in range(LR):
                        parts = row_parts([w[i] * pat[r][i] for i in range(3)], lane)
                        sums = [
                            jnp.broadcast_to(jnp.sum(p, axis=1, keepdims=True), (8, LANES))
                            for p in parts
                        ]
                        for j in range(4):
                            proj[r] = jnp.where(lane == 4 * g + j, sums[j], proj[r])
                        if full:
                            acc[r][0] += w[0] * jnp.where(lane < 96, sums[0], sums[1])
                            acc[r][1] += w[1] * jnp.where(lane < 64, sums[1], sums[2])
                            acc[r][2] += w[2] * jnp.where(lane < 32, sums[2], sums[3])
                return tuple(proj), tuple(tuple(a) for a in acc)

            start = ((zero,) * LR, ((zero,) * 3,) * LR)
            proj, acc = lax.fori_loop(0, GROUPS // UNROLL, step, start)
            for r in range(LR):
                dst[pl.ds(pl.multiple_of(dst_base + r * NBLK + 8 * t, 8), 8), :] = proj[r]
                if full:
                    a = acc[r]
                    total = (
                        a[0]
                        + pltpu.roll(jnp.where(lane >= 96, a[0], a[1]), 32, 1)
                        + pltpu.roll(jnp.where(lane >= 64, a[1], a[2]), 64, 1)
                        + pltpu.roll(a[2], 96, 1)
                    )
                    ext[slot, pl.ds(pl.multiple_of(r * EXT + 8 * t, 8), 8), :] = x[r] + jnp.where(
                        lane < 96, total, zero
                    )
            return 0

        lax.fori_loop(0, TILES, tile, 0)

    def halo_copies(h):
        return (
            pltpu.make_async_remote_copy(
                src_ref=hsend.at[h, 0], dst_ref=hrecv.at[h, 1],
                send_sem=hs_sem.at[h, 0], recv_sem=hr_sem.at[h, 1],
                device_id={"sub": before}, device_id_type=MESH,
            ),
            pltpu.make_async_remote_copy(
                src_ref=hsend.at[h, 1], dst_ref=hrecv.at[h, 0],
                send_sem=hs_sem.at[h, 1], recv_sem=hr_sem.at[h, 0],
                device_id={"sub": after}, device_id_type=MESH,
            ),
        )

    def halo_start(h, slot):
        for side in range(2):
            for j in range(IF):
                idx = send_ref[0, side * IF + j]
                for r in range(LR):
                    hsend[h, side, pl.ds(r * 8 + j, 1), :] = ext[slot, pl.ds(r * EXT + idx, 1), :]
        for copy in halo_copies(h):
            copy.start()

    def halo_finish(h, slot):
        for copy in halo_copies(h):
            copy.wait_recv()
        for side in range(2):
            edge = jnp.where(sub == (0 if side == 0 else nsub - 1), 0, 1)
            inside = jnp.broadcast_to(edge, (8, LANES)) > 0
            for r in range(LR):
                v = hrecv[h, side, pl.ds(r * 8, 8), :]
                ext[slot, pl.ds(r * EXT + NBLK + 8 * side, 8), :] = jnp.where(
                    inside, v, jnp.zeros_like(v)
                )

    def halo_sent(h):
        for copy in halo_copies(h):
            copy.wait_send()

    def stiffness(slot, dst):
        def gather(s, _):
            for q in range(4):
                n = s * 4 + q
                for k in range(1, K):
                    c = colx[n * K + k]
                    for r in range(LR):
                        gat[pl.ds(((k - 1) * LR + r) * NBLK + n, 1), :] = ext[
                            slot, pl.ds(r * EXT + c, 1), :
                        ]
            return 0

        lax.fori_loop(0, NBLK // 4, gather, 0)

        def tile(t, _):
            pat = []
            for r in range(LR):
                own = ext[slot, pl.ds(pl.multiple_of(r * EXT + 8 * t, 8), 8), :]
                rest = [
                    gat[pl.ds(pl.multiple_of(((k - 1) * LR + r) * NBLK + 8 * t, 8), 8), :]
                    for k in range(1, K)
                ]
                pat.append([patterns(v, lane) for v in [own] + rest])
            zero = jnp.zeros((8, LANES), jnp.float32)

            def step(s, out):
                out = list(out)
                for q in range(UNROLL):
                    g = s * UNROLL + q
                    prod = [[None] * 3 for _ in range(LR)]
                    for i in range(3):
                        a = [blocks[t, 3 * g + i, k] for k in range(K)]
                        for r in range(LR):
                            prod[r][i] = (a[0] * pat[r][0][i] + a[1] * pat[r][1][i]) + (
                                a[2] * pat[r][2][i] + a[3] * pat[r][3][i]
                            )
                    for r in range(LR):
                        for j, p in enumerate(row_parts(prod[r], lane)):
                            s_j = jnp.broadcast_to(jnp.sum(p, axis=1, keepdims=True), (8, LANES))
                            out[r] = jnp.where(lane == 4 * g + j, s_j, out[r])
                return tuple(out)

            out = lax.fori_loop(0, GROUPS // UNROLL, step, (zero,) * LR)
            for r in range(LR):
                dst[pl.ds(pl.multiple_of(r * NBLK + 8 * t, 8), 8), :] = out[r]
            return 0

        lax.fori_loop(0, TILES, tile, 0)

    def stage_copy(buf, ssem, rsem, rd, d, mine, target):
        at = rd * 8 + mine
        return pltpu.make_async_remote_copy(
            src_ref=buf.at[at], dst_ref=buf.at[at],
            send_sem=ssem.at[rd * 8 + d], recv_sem=rsem.at[at],
            device_id={"sub": target}, device_id_type=MESH,
        )

    def arrived(buf, ssem, rsem, rd, d, source, target):
        at = rd * 8 + source
        pltpu.make_async_remote_copy(
            src_ref=buf.at[at], dst_ref=buf.at[at],
            send_sem=ssem.at[rd * 8 + d], recv_sem=rsem.at[at],
            device_id={"sub": target}, device_id_type=MESH,
        ).wait_recv()

    def sum_start(rd, pairs):
        tiles = []
        srow = lax.broadcasted_iota(jnp.int32, (8, LANES), 0)
        for r in range(LR):
            tile = jnp.zeros((8, LANES), jnp.float32)
            for d, (a, b) in enumerate(pairs):
                row = jnp.sum(a[r] * b[r], axis=0, keepdims=True)
                tile = jnp.where(srow == d, jnp.broadcast_to(row, (8, LANES)), tile)
            tiles.append(jnp.sum(tile, axis=1, keepdims=True))
        rb1[rd * 8 + spot] = jnp.where(
            lane < 64,
            jnp.broadcast_to(tiles[0], (8, LANES)),
            jnp.broadcast_to(tiles[1], (8, LANES)),
        )
        for d in range(1, PLANE):
            stage_copy(rb1, r1s, r1r, rd, d, spot, in_plane(d)).start()

    def sum_middle(rd):
        for d in range(1, PLANE):
            arrived(rb1, r1s, r1r, rd, d, lax.rem(spot + d, PLANE), in_plane(d))
        v = [rb1[rd * 8 + s] for s in range(PLANE)]
        rb2[rd * 8 + plane] = ((v[0] + v[1]) + (v[2] + v[3])) + ((v[4] + v[5]) + (v[6] + v[7]))
        for d in range(1, planes):
            stage_copy(rb2, r2s, r2r, rd, d, plane, across(d)).start()

    def sum_finish(rd):
        for d in range(1, planes):
            arrived(rb2, r2s, r2r, rd, d, lax.rem(plane + d, planes), across(d))
        v = rb2[rd * 8]
        for s in range(1, planes):
            v = v + rb2[rd * 8 + s]
        swapped = pltpu.roll(v, 64, 1)
        for d in range(1, PLANE):
            stage_copy(rb1, r1s, r1r, rd, d, spot, in_plane(d)).wait_send()
        for d in range(1, planes):
            stage_copy(rb2, r2s, r2r, rd, d, plane, across(d)).wait_send()
        return (jnp.where(lane < 64, v, swapped), jnp.where(lane < 64, swapped, v))

    def factor_row(src, j, kind):
        return pl.multiple_of(((src * ITERS + j) * 2 + kind) * VEC, 8)

    def factor_copy(buf, left, j, kind, d, src, target):
        at = factor_row(src, j, kind)
        piece = (j * 2 + left) * 2 + kind
        return pltpu.make_async_remote_copy(
            src_ref=buf.at[pl.ds(at, VEC), :], dst_ref=buf.at[pl.ds(at, VEC), :],
            send_sem=fs_sem.at[piece * 4 + d], recv_sem=fr_sem.at[piece * 4 + src],
            device_id={"rhs": target}, device_id_type=MESH,
        )

    def factor_send(buf, left, j, kind):
        for d in range(1, nrhs):
            factor_copy(buf, left, j, kind, d, me, lax.rem(me + d, nrhs)).start()

    def rows(ref, i):
        return [
            ref[pl.ds(pl.multiple_of(i * VEC + r * NBLK, 8), NBLK), :] for r in range(LR)
        ]

    def put(ref, i, v):
        for r in range(LR):
            ref[pl.ds(pl.multiple_of(i * VEC + r * NBLK, 8), NBLK), :] = v[r]

    def put_at(ref, base, v):
        for r in range(LR):
            ref[pl.ds(pl.multiple_of(base + r * NBLK, 8), NBLK), :] = v[r]

    def ext_rows(slot):
        return [ext[slot, pl.ds(r * EXT, NBLK), :] for r in range(LR)]

    def axpy(x, s, y):
        return [a + c * b for a, c, b in zip(x, s, y)]

    def scale(s, y):
        return [c * b for c, b in zip(s, y)]

    def keep(kind, i, v):
        for r in range(LR):
            scr[pl.ds((r * 6 + kind) * ITERS + i, 1), :] = v[r]

    def kept(kind, i):
        return [scr[pl.ds((r * 6 + kind) * ITERS + i, 1), :] for r in range(LR)]

    pre_copy.wait()
    precondition(rh, 0, uh, 0, 0)
    pl.semaphore_wait(barrier, peers)
    halo_start(0, 0)
    put(zh, 0, ext_rows(0))
    precondition(tvec, 0, utv, 0, 1)
    halo_start(1, 1)
    put(tmv, 0, ext_rows(1))
    for t in range(TILES):
        stiff_copies[t].wait()

        def relay(s, _, t=t):
            for q in range(4):
                c = s * 4 + q
                for k in range(K):
                    blocks[t, c, k] = raw[t, pl.ds(c * K + k, 8, stride=CHUNKS * K), :]
            return 0

        lax.fori_loop(0, CHUNKS // 4, relay, 0)
    halo_finish(0, 0)
    stiffness(0, nvec)
    put(wh, 0, rows(nvec, 0))
    halo_finish(1, 1)
    stiffness(1, atv)
    halo_sent(0)
    halo_sent(1)

    def forward(i, carry):
        rho_old, gamma_old, c_old = carry[:3]
        z, w, res, t = rows(zh, i), rows(wh, i), rows(rh, i), rows(tvec, 0)
        q_old, s_old = rows(qh, i), rows(sh, i)
        sum_start(
            i,
            (
                (res, z), (z, w), (z, q_old), (t, z),
                (t, s_old), (w, s_old), (q_old, s_old),
            ),
        )
        precondition(wh, i * VEC, hvec, 0, 0)
        halo_start(2 + i, 0)
        at = factor_row(me, i, 0)
        put_at(fl, at, rows(uh, i))
        at = factor_row(me, i, 1)
        put_at(fr, at, rows(rh, i))
        factor_send(fl, 1, i, 0)
        factor_send(fr, 0, i, 1)
        sum_middle(i)
        halo_finish(2 + i, 0)
        stiffness(0, nvec)
        halo_sent(2 + i)
        tot = sum_finish(i)
        val = [[tot[r][d : d + 1, :] for r in range(LR)] for d in range(7)]
        rho, za, zq, tz = val[:4]
        first = jnp.broadcast_to(jnp.where(i == 0, 1, 0), (1, LANES)) > 0
        beta = [jnp.where(first, 0.0, a / b) for a, b in zip(rho, rho_old)]
        gamma = [
            za[r] + beta[r] * (2.0 * zq[r] + beta[r] * gamma_old[r]) for r in range(LR)
        ]
        c = axpy(tz, beta, c_old)
        alpha = [a / b for a, b in zip(rho, gamma)]
        minus = [-a for a in alpha]
        for kind, v in enumerate((alpha, gamma, rho, beta, c, zq)):
            keep(kind, i, v)
        p = axpy(rows(zh, i), beta, rows(ph, i))
        put(ph, i + 1, p)
        put(xv, 0, axpy(rows(xv, 0), alpha, p))
        q = axpy(rows(wh, i), beta, rows(qh, i))
        put(qh, i + 1, q)
        put(rh, i + 1, axpy(rows(rh, i), minus, q))
        s = axpy(ext_rows(0), beta, rows(sh, i))
        put(sh, i + 1, s)
        put(zh, i + 1, axpy(rows(zh, i), minus, s))
        y = axpy(rows(nvec, 0), beta, rows(yv, 0))
        put(yv, 0, y)
        put(wh, i + 1, axpy(rows(wh, i), minus, y))
        k = axpy(rows(hvec, 0), beta, rows(kv, 0))
        put(kv, 0, k)
        put(uh, i + 1, axpy(rows(uh, i), minus, k))
        return (
            tuple(rho), tuple(gamma), tuple(c),
            tuple(val[4]), tuple(val[5]), tuple(val[6]),
        )

    none = (jnp.zeros((1, LANES), jnp.float32),) * LR
    one = (jnp.ones((1, LANES), jnp.float32),) * LR
    last = lax.fori_loop(0, ITERS, forward, (one, none, none, none, none, none))
    gamma3, c3, ts, ws, qs = last[1:]

    def adjoint(i, bb, e0, e1, norm_bar, pb, wp, mp, amp):
        ratio = [a / b for a, b in zip(bb, kept(2, i))]
        full = [a + b for a, b in zip(norm_bar, ratio)]
        twice = [2.0 * a for a in full]
        zq, beta = kept(5, i + 1), kept(3, i + 1)
        err = [e0[r] + twice[r] * zq[r] + e1[r] for r in range(LR)]
        put_at(fr, factor_row(me, i + 1, 0), axpy(pb, full, rows(rh, i + 1)))
        put_at(fl, factor_row(me, i + 1, 1), axpy(wp, full, rows(uh, i + 1)))
        factor_send(fr, 0, i + 1, 0)
        factor_send(fl, 1, i + 1, 1)
        rb = axpy([a + b for a, b in zip(rows(rbv, 0), mp)], twice, rows(zh, i + 1))
        put(rbv, 0, rb)
        arb = axpy([a + b for a, b in zip(rows(arbv, 0), amp)], twice, rows(wh, i + 1))
        put(arbv, 0, arb)
        alpha, gamma = kept(0, i), kept(1, i)
        step_bar = [a - b for a, b in zip(kept(4, i), err)]
        curv2 = [-2.0 * (s * a / g) for s, a, g in zip(step_bar, alpha, gamma)]
        norm_bar = [s / g - a * b for s, g, a, b in zip(step_bar, gamma, ratio, beta)]
        diff = [a - b for a, b in zip(rows(tvec, 0), arb)]
        pb = axpy(axpy(scale(beta, pb), alpha, diff), curv2, rows(qh, i + 1))
        put(pbv, 0, pb)
        return tuple(norm_bar)

    alpha3, beta3, zq3 = kept(0, 3), kept(3, 3), kept(5, 3)
    gamma2, c2 = kept(1, 2), kept(4, 2)
    g2 = [-2.0 * (c * a / g) for c, a, g in zip(c3, alpha3, gamma3)]
    mix = lambda a, b: axpy(scale(alpha3, a), g2, b)
    bb = [
        alpha3[r] * c2[r] + g2[r] * (zq3[r] + beta3[r] * gamma2[r]) for r in range(LR)
    ]
    e1 = [alpha3[r] * ts[r] + g2[r] * (ws[r] + beta3[r] * qs[r]) for r in range(LR)]
    norm_bar = adjoint(
        2, bb, none, e1, [c / g for c, g in zip(c3, gamma3)],
        mix(rows(tvec, 0), rows(qh, 4)),
        mix(rows(utv, 0), rows(kv, 0)),
        mix(rows(tmv, 0), rows(sh, 4)),
        mix(rows(atv, 0), rows(yv, 0)),
    )

    def backward(it, norm_bar):
        i = 1 - it
        rd = ITERS + it
        pb = rows(pbv, 0)
        sum_start(
            rd,
            (
                (pb, rows(ph, i + 1)),
                (rows(rbv, 0), rows(qh, i + 1)),
                (pb, rows(sh, i + 1)),
            ),
        )
        precondition(pbv, 0, hvec, 0, 0)
        halo_start(2 + rd, 0)
        sum_middle(rd)
        halo_finish(2 + rd, 0)
        stiffness(0, nvec)
        halo_sent(2 + rd)
        tot = sum_finish(rd)
        bb, e0, e1 = [[tot[r][d : d + 1, :] for r in range(LR)] for d in range(3)]
        return adjoint(
            i, bb, e0, e1, norm_bar,
            rows(pbv, 0), rows(hvec, 0), ext_rows(0), rows(nvec, 0),
        )

    norm_bar = lax.fori_loop(0, 2, backward, norm_bar)

    zeta = factor_row(me, 0, 0)
    put_at(fr, zeta, axpy(rows(pbv, 0), norm_bar, rows(rh, 0)))
    factor_send(fr, 0, 0, 0)
    precondition(fr, zeta, fl, factor_row(me, 0, 1), None)
    factor_send(fl, 1, 0, 1)

    for r in range(LR):
        parts = [xv[pl.ds(r * NBLK + j, 12, stride=4), :] for j in range(4)]
        for i, chunk in enumerate(rows_to_chunks(parts, lane12)):
            sol_ref[pl.ds(2 * i + r, 12, stride=6), :] = chunk

    def factors_wait(j, _):
        for left, buf in ((1, fl), (0, fr)):
            for kind in range(2):
                for d in range(1, nrhs):
                    src = lax.rem(me + d, nrhs)
                    factor_copy(buf, left, j, kind, d, src, src).wait_recv()
                    factor_copy(buf, left, j, kind, d, me, src).wait_send()
        return 0

    lax.fori_loop(0, ITERS, factors_wait, 0)

    depth = nrhs * ITERS * 2 * LR
    lane24 = lax.broadcasted_iota(jnp.int32, (24, LANES), 1)

    def halves(v):
        hi = v.astype(jnp.bfloat16)
        return hi, (v - hi.astype(jnp.float32)).astype(jnp.bfloat16)

    def out_copy(t):
        span = pl.ds(pl.multiple_of(t * CHUNKS * 8, 8), CHUNKS * 8)
        return pltpu.make_async_copy(go.at[span, :], grad_hbm.at[span, :], out_sem.at[t])

    def grads(t, _):
        for s in range(8):
            n = t * 8 + s
            lh, ll = halves(fl[pl.ds(n, depth, stride=NBLK), :])
            rhi, rlo = halves(fr[pl.ds(n, depth, stride=NBLK), :])
            gb[s] = lax.dot_general(
                jnp.concatenate([lh, lh, ll], axis=0),
                jnp.concatenate([rhi, rlo, rhi], axis=0),
                (((0,), (0,)), ((), ())),
                preferred_element_type=jnp.float32,
            )
            parts = [gb[s, pl.ds(j, 24, stride=4), :] for j in range(4)]
            for i, chunk in enumerate(rows_to_chunks(parts, lane24)):
                go[pl.ds(t * (CHUNKS * 8) + i * 8 + s, 24, stride=24), :] = chunk
        out_copy(t).start()
        return 0

    lax.fori_loop(0, TILES, grads, 0)
    for t in range(TILES):
        out_copy(t).wait()


def shards(planes, nrhs, stiffness, precond, rhs_vec, cotangent, col_index, send_rows, counts):
    def flat(v):
        return v.reshape(LR, ROWS // LR, LANES).transpose(1, 0, 2).reshape(ROWS, LANES)

    stiff = stiffness.reshape(NBLK, K, CHUNKS, LANES).transpose(0, 2, 1, 3)
    stiff = stiff.reshape(TILES, 8 * CHUNKS * K, LANES)
    pre = precond.reshape(TILES, 8, CHUNKS, LANES).transpose(0, 2, 1, 3)
    f32 = jnp.float32
    vmem = pl.BlockSpec(memory_space=pltpu.VMEM)
    smem = pl.BlockSpec(memory_space=pltpu.SMEM)
    hbm = pl.BlockSpec(memory_space=pl.ANY)

    def vec(count=1):
        return pltpu.VMEM((count * VEC, LANES), f32)

    dma = pltpu.SemaphoreType.DMA
    factors = nrhs * ITERS * 2 * VEC
    sol, grad = pl.pallas_call(
        functools.partial(kernel, planes, nrhs),
        out_shape=(
            jax.ShapeDtypeStruct((ROWS, LANES), f32),
            jax.ShapeDtypeStruct((TILES * CHUNKS * 8, LANES), f32),
        ),
        in_specs=[smem, smem, smem, vmem, vmem, hbm, hbm],
        out_specs=(vmem, hbm),
        scratch_shapes=[
            pltpu.VMEM((TILES, 8 * CHUNKS * K, LANES), f32),
            pltpu.VMEM((TILES, CHUNKS, K, 8, LANES), f32),
            pltpu.VMEM((TILES, CHUNKS, 8, LANES), f32),
            pltpu.SMEM((NBLK * K,), jnp.int32),
            pltpu.VMEM((2, LR * EXT, LANES), f32),
            vec(K - 1),
        ]
        + [vec() for _ in range(9)]
        + [vec() for _ in range(3)]
        + [vec(ITERS + 1) for _ in range(7)]
        + [
            pltpu.VMEM((LR * 6 * ITERS, LANES), f32),
            pltpu.VMEM((HALOS, 2, LR * 8, LANES), f32),
            pltpu.VMEM((HALOS, 2, LR * 8, LANES), f32),
            pltpu.VMEM((REDS * 8, 8, LANES), f32),
            pltpu.VMEM((REDS * 8, 8, LANES), f32),
            pltpu.VMEM((factors, LANES), f32),
            pltpu.VMEM((factors, LANES), f32),
            pltpu.VMEM((8, LANES, LANES), f32),
            pltpu.VMEM((TILES * CHUNKS * 8, LANES), f32),
            dma((TILES + 1,)),
            dma((TILES,)),
            dma((HALOS, 2)),
            dma((HALOS, 2)),
            dma((REDS * 8,)),
            dma((REDS * 8,)),
            dma((REDS * 8,)),
            dma((REDS * 8,)),
            dma((ITERS * 16,)),
            dma((ITERS * 16,)),
        ],
        compiler_params=pltpu.CompilerParams(
            collective_id=0, has_side_effects=True, vmem_limit_bytes=48 * 1024 * 1024
        ),
        name="cg_adjoint",
    )(col_index, send_rows, counts, flat(rhs_vec), flat(cotangent), stiff, pre)
    sol = sol.reshape(ROWS // LR, LR, LANES).transpose(1, 0, 2).reshape(LR, NBLK * BS)
    grad = grad.reshape(TILES, CHUNKS, 8, LANES).transpose(0, 2, 1, 3)
    return sol, grad.reshape(NBLK, BS * BS)


def solution(mesh):
    in_specs = (
        P("sub", None, None),
        P("sub", None),
        P("rhs", "sub"),
        P("rhs", "sub"),
        P("sub", None),
        P("sub", None),
        P("sub"),
    )
    out_specs = (P("rhs", "sub"), P("sub", None))
    body = functools.partial(shards, mesh.shape["sub"] // PLANE, mesh.shape["rhs"])
    return jax.shard_map(body, mesh=mesh, in_specs=in_specs, out_specs=out_specs, check_vma=False)
```

```python
import functools

import jax
import jax.numpy as jnp
from jax import lax
from jax.experimental import pallas as pl
from jax.experimental.pallas import tpu as pltpu
from jax.sharding import PartitionSpec as P

BS = 96
K = 4
NBLK = 48
IF = 6
ITERS = 4
LR = 2
LANES = 128
TILES = NBLK // 8
CHUNKS = BS * BS // LANES
VEC = LR * NBLK
ROWS = LR * BS * NBLK // LANES
GROUPS = CHUNKS // 3
SPAN = 24
HALOS = 8
REDS = 6
EXT = 64
MESH = pl.DeviceIdType.MESH


def lane_iota():
    return lax.broadcasted_iota(jnp.int32, (8, LANES), 1)


def patterns(x, lane):
    far = pltpu.roll(x, 96, 1)
    mid = pltpu.roll(x, 64, 1)
    near = pltpu.roll(x, 32, 1)
    return (
        jnp.where(lane < 96, x, far),
        jnp.where(lane < 64, far, mid),
        jnp.where(lane < 32, mid, near),
    )


def row_parts(p, lane):
    zero = jnp.zeros_like(p[0])
    return (
        jnp.where(lane < 96, p[0], zero),
        jnp.where(lane < 64, p[1], jnp.where(lane >= 96, p[0], zero)),
        jnp.where(lane >= 64, p[1], jnp.where(lane < 32, p[2], zero)),
        jnp.where(lane >= 32, p[2], zero),
    )


def rows_to_chunks(r, lane):
    far = pltpu.roll(r[1], 96, 1)
    mid = pltpu.roll(r[2], 64, 1)
    return (
        jnp.where(lane < 96, r[0], far),
        jnp.where(lane < 64, far, mid),
        jnp.where(lane < 32, mid, pltpu.roll(r[3], 32, 1)),
    )


def chunks_to_rows(c, lane):
    zero = jnp.zeros_like(c[0])
    rows = (
        c[0],
        pltpu.roll(jnp.where(lane >= 96, c[0], c[1]), 32, 1),
        pltpu.roll(jnp.where(lane >= 64, c[1], c[2]), 64, 1),
        pltpu.roll(c[2], 96, 1),
    )
    return [jnp.where(lane < 96, r, zero) for r in rows]


def kernel(
    nsub, nrhs,
    col_hbm, send_hbm, count_hbm, rhs_ref, cot_ref, stiff_hbm, pre_hbm,
    sol_ref, go,
    colx, sendx, countx, flat, blocks, weights, ext, gat,
    nvec, hvec, tvec, tmv, utv, atv, yv, kv, xv, pbv, rbv, arbv,
    ph, qh, sh, zh, wh, rh, uh, scr, hsend, hrecv, rbuf, fl, fr, gb,
    load_sem, small_sem, hs_sem, hr_sem, rs_sem, rr_sem, fs_sem, fr_sem,
):
    sub = lax.axis_index("sub")
    me = lax.axis_index("rhs")
    lane = lane_iota()
    f32, bf16 = jnp.float32, jnp.bfloat16

    small = [
        pltpu.make_async_copy(col_hbm, colx, small_sem.at[0]),
        pltpu.make_async_copy(send_hbm, sendx, small_sem.at[1]),
        pltpu.make_async_copy(count_hbm, countx, small_sem.at[2]),
    ]
    pre_copies = [
        pltpu.make_async_copy(
            pre_hbm.at[t], weights.at[:, pl.ds(8 * t, 8), :], load_sem.at[NBLK + t]
        )
        for t in range(TILES)
    ]
    for copy in small + pre_copies:
        copy.start()

    def stiff_copy(n):
        return pltpu.make_async_copy(stiff_hbm.at[n], blocks.at[:, :, n, :], load_sem.at[n])

    for n in range(NBLK):
        stiff_copy(n).start()

    barrier = pltpu.get_barrier_semaphore()

    def greet(d, _):
        pl.semaphore_signal(
            barrier, inc=1, device_id={"sub": lax.rem(sub + d, nsub)}, device_id_type=MESH
        )
        return 0

    lax.fori_loop(1, nsub, greet, 0)
    for d in range(1, nrhs):
        pl.semaphore_signal(
            barrier, inc=1, device_id={"rhs": lax.rem(me + d, nrhs)}, device_id_type=MESH
        )
    peers = nsub - 1 + nrhs - 1
    before = lax.rem(sub + nsub - 1, nsub)
    after = lax.rem(sub + 1, nsub)

    hsend[...] = jnp.zeros_like(hsend)
    for ref in (ph, qh, sh):
        ref[pl.ds(0, VEC), :] = jnp.zeros((VEC, LANES), f32)
    for ref in (yv, kv, xv, rbv, arbv):
        ref[...] = jnp.zeros_like(ref)
    for copy in small:
        copy.wait()
    for n in range(NBLK):
        for k in range(1, K):
            c = colx[k, n]
            colx[k, n] = jnp.where(
                c < IF, c + NBLK, jnp.where(c < IF + NBLK, c - IF, c + 8 - IF)
            )

    lane12 = lax.broadcasted_iota(jnp.int32, (12, LANES), 1)
    row12 = lax.broadcasted_iota(jnp.int32, (12, LANES), 0)
    live = countx[0]
    for c in range(ROWS // LR):
        flat[0, pl.ds(LR * c, LR), :] = rhs_ref[:, pl.ds(c * LANES, LANES)]
        flat[1, pl.ds(LR * c, LR), :] = cot_ref[:, pl.ds(c * LANES, LANES)]
    for r in range(LR):
        chunks = [flat[0, pl.ds(2 * i + r, 12, stride=6), :] for i in range(3)]
        for j, row in enumerate(chunks_to_rows(chunks, lane12)):
            row = jnp.where(row12 * 4 + j < live, row, jnp.zeros_like(row))
            rh[pl.ds(r * NBLK + j, 12, stride=4), :] = row
        chunks = [flat[1, pl.ds(2 * i + r, 12, stride=6), :] for i in range(3)]
        for j, row in enumerate(chunks_to_rows(chunks, lane12)):
            tvec[pl.ds(r * NBLK + j, 12, stride=4), :] = row

    def halves(v):
        hi = v.astype(bf16)
        return hi, (v - hi.astype(f32)).astype(bf16)

    def row_sums(v):
        return [
            jnp.broadcast_to(jnp.sum(p, axis=1, keepdims=True), (8, LANES))
            for p in row_parts(v, lane)
        ]

    def precondition(src, base, dst, dst_base, slot):
        full = slot is not None

        def tile(t, _):
            at = pl.multiple_of(8 * t, 8)
            x = [src[pl.ds(pl.multiple_of(base + r * NBLK + 8 * t, 8), 8), :] for r in range(LR)]
            pat = [patterns(v, lane) for v in x]
            zero = jnp.zeros((8, LANES), f32)

            def step(s, carry):
                proj, acc = carry
                proj, acc = list(proj), [list(a) for a in acc]
                for q in range(SPAN):
                    g = s * SPAN + q
                    w = [weights[3 * g + i, pl.ds(at, 8), :] for i in range(3)]
                    for r in range(LR):
                        sums = row_sums([w[i] * pat[r][i] for i in range(3)])
                        for j in range(4):
                            proj[r] = jnp.where(lane == 4 * g + j, sums[j], proj[r])
                        if full:
                            acc[r][0] += w[0] * jnp.where(lane < 96, sums[0], sums[1])
                            acc[r][1] += w[1] * jnp.where(lane < 64, sums[1], sums[2])
                            acc[r][2] += w[2] * jnp.where(lane < 32, sums[2], sums[3])
                return tuple(proj), tuple(tuple(a) for a in acc)

            carry = ((zero,) * LR, ((zero,) * 3,) * LR)
            if SPAN == GROUPS:
                proj, acc = step(0, carry)
            else:
                proj, acc = lax.fori_loop(0, GROUPS // SPAN, step, carry)
            for r in range(LR):
                dst[pl.ds(pl.multiple_of(dst_base + r * NBLK + 8 * t, 8), 8), :] = proj[r]
                if full:
                    a = acc[r]
                    total = (
                        a[0]
                        + pltpu.roll(jnp.where(lane >= 96, a[0], a[1]), 32, 1)
                        + pltpu.roll(jnp.where(lane >= 64, a[1], a[2]), 64, 1)
                        + pltpu.roll(a[2], 96, 1)
                    )
                    ext[slot, pl.ds(pl.multiple_of(r * EXT + 8 * t, 8), 8), :] = x[r] + jnp.where(
                        lane < 96, total, zero
                    )
            return 0

        lax.fori_loop(0, TILES, tile, 0)

    def halo_copies(h):
        return (
            pltpu.make_async_remote_copy(
                src_ref=hsend.at[h, 0], dst_ref=hrecv.at[h, 1],
                send_sem=hs_sem.at[h, 0], recv_sem=hr_sem.at[h, 1],
                device_id={"sub": before}, device_id_type=MESH,
            ),
            pltpu.make_async_remote_copy(
                src_ref=hsend.at[h, 1], dst_ref=hrecv.at[h, 0],
                send_sem=hs_sem.at[h, 1], recv_sem=hr_sem.at[h, 0],
                device_id={"sub": after}, device_id_type=MESH,
            ),
        )

    def halo_start(h, slot):
        for side in range(2):
            for j in range(IF):
                idx = sendx[0, side * IF + j]
                for r in range(LR):
                    hsend[h, side, pl.ds(r * 8 + j, 1), :] = ext[slot, pl.ds(r * EXT + idx, 1), :]
        for copy in halo_copies(h):
            copy.start()

    def halo_finish(h, slot):
        for copy in halo_copies(h):
            copy.wait_recv()
        for side in range(2):
            edge = jnp.where(sub == (0 if side == 0 else nsub - 1), 0, 1)
            inside = jnp.broadcast_to(edge, (8, LANES)) > 0
            for r in range(LR):
                v = hrecv[h, side, pl.ds(r * 8, 8), :]
                ext[slot, pl.ds(r * EXT + NBLK + 8 * side, 8), :] = jnp.where(
                    inside, v, jnp.zeros_like(v)
                )

    def halo_sent(h):
        for copy in halo_copies(h):
            copy.wait_send()

    def stiffness(slot, dst):
        def gather(s, _):
            for q in range(4):
                n = s * 4 + q
                for k in range(1, K):
                    c = colx[k, n]
                    for r in range(LR):
                        gat[pl.ds(((k - 1) * LR + r) * NBLK + n, 1), :] = ext[
                            slot, pl.ds(r * EXT + c, 1), :
                        ]
            return 0

        lax.fori_loop(0, NBLK // 4, gather, 0)

        def tile(t, _):
            at = pl.multiple_of(8 * t, 8)
            pat = []
            for r in range(LR):
                own = ext[slot, pl.ds(pl.multiple_of(r * EXT + 8 * t, 8), 8), :]
                rest = [
                    gat[pl.ds(pl.multiple_of(((k - 1) * LR + r) * NBLK + 8 * t, 8), 8), :]
                    for k in range(1, K)
                ]
                pat.append([patterns(v, lane) for v in [own] + rest])

            def step(s, out):
                out = list(out)
                for q in range(SPAN):
                    g = s * SPAN + q
                    prod = [[None] * 3 for _ in range(LR)]
                    for i in range(3):
                        a = [blocks[3 * g + i, k, pl.ds(at, 8), :] for k in range(K)]
                        for r in range(LR):
                            prod[r][i] = (a[0] * pat[r][0][i] + a[1] * pat[r][1][i]) + (
                                a[2] * pat[r][2][i] + a[3] * pat[r][3][i]
                            )
                    for r in range(LR):
                        for j, v in enumerate(row_sums(prod[r])):
                            out[r] = jnp.where(lane == 4 * g + j, v, out[r])
                return tuple(out)

            out = (jnp.zeros((8, LANES), f32),) * LR
            if SPAN == GROUPS:
                out = step(0, out)
            else:
                out = lax.fori_loop(0, GROUPS // SPAN, step, out)
            for r in range(LR):
                dst[pl.ds(pl.multiple_of(r * NBLK + 8 * t, 8), 8), :] = out[r]
            return 0

        lax.fori_loop(0, TILES, tile, 0)

    def sum_copy(rd, d):
        at = rd * nsub + sub
        return pltpu.make_async_remote_copy(
            src_ref=rbuf.at[at], dst_ref=rbuf.at[at],
            send_sem=rs_sem.at[rd], recv_sem=rr_sem.at[rd],
            device_id={"sub": lax.rem(sub + d, nsub)}, device_id_type=MESH,
        )

    srow = lax.broadcasted_iota(jnp.int32, (8, LANES), 0)

    def sum_start(rd, pairs):
        payload = jnp.zeros((8, LANES), f32)
        for r in range(LR):
            tile = jnp.zeros((8, LANES), f32)
            for d, (a, b) in enumerate(pairs):
                row = jnp.sum(a[r] * b[r], axis=0, keepdims=True)
                tile = jnp.where(srow == d, jnp.broadcast_to(row, (8, LANES)), tile)
            tot = jnp.broadcast_to(jnp.sum(tile, axis=1, keepdims=True), (8, LANES))
            payload = jnp.where(lane == srow + 64 * r, tot, payload)
        rbuf[rd * nsub + sub] = jnp.sum(payload, axis=0, keepdims=True)

        def send(d, _):
            sum_copy(rd, d).start()
            return 0

        lax.fori_loop(1, nsub, send, 0)

    def sum_finish(rd):
        span = rbuf.at[pl.ds(rd * nsub, nsub - 1)]
        pltpu.make_async_copy(span, span, rr_sem.at[rd]).wait()
        parts = [jnp.zeros((1, LANES), f32)] * 4
        for s in range(nsub):
            parts[s % 4] = parts[s % 4] + rbuf[rd * nsub + s]
        row = jnp.broadcast_to((parts[0] + parts[1]) + (parts[2] + parts[3]), (8, LANES))
        pltpu.make_async_copy(span, span, rs_sem.at[rd]).wait()
        return [
            jnp.broadcast_to(
                jnp.sum(
                    jnp.where(lane == srow + 64 * r, row, jnp.zeros_like(row)),
                    axis=1, keepdims=True,
                ),
                (8, LANES),
            )
            for r in range(LR)
        ]

    def factor_row(src, j, kind):
        return pl.multiple_of(((src * ITERS + j) * 2 + kind) * VEC, 8)

    def factor_copy(buf, left, j, kind, d, src, target):
        at = factor_row(src, j, kind)
        piece = (j * 2 + left) * 2 + kind
        return pltpu.make_async_remote_copy(
            src_ref=buf.at[pl.ds(at, VEC), :], dst_ref=buf.at[pl.ds(at, VEC), :],
            send_sem=fs_sem.at[piece * 4 + d], recv_sem=fr_sem.at[piece * 4 + src],
            device_id={"rhs": target}, device_id_type=MESH,
        )

    def factor_send(buf, left, j, kind):
        for d in range(1, nrhs):
            factor_copy(buf, left, j, kind, d, me, lax.rem(me + d, nrhs)).start()

    def rows(ref, i):
        return [
            ref[pl.ds(pl.multiple_of(i * VEC + r * NBLK, 8), NBLK), :] for r in range(LR)
        ]

    def put(ref, i, v):
        for r in range(LR):
            ref[pl.ds(pl.multiple_of(i * VEC + r * NBLK, 8), NBLK), :] = v[r]

    def put_at(ref, base, v):
        for r in range(LR):
            ref[pl.ds(pl.multiple_of(base + r * NBLK, 8), NBLK), :] = v[r]

    def ext_rows(slot):
        return [ext[slot, pl.ds(r * EXT, NBLK), :] for r in range(LR)]

    def axpy(x, s, y):
        return [a + c * b for a, c, b in zip(x, s, y)]

    def scale(s, y):
        return [c * b for c, b in zip(s, y)]

    def keep(kind, i, v):
        for r in range(LR):
            scr[pl.ds((r * 6 + kind) * ITERS + i, 1), :] = v[r]

    def kept(kind, i):
        return [scr[pl.ds((r * 6 + kind) * ITERS + i, 1), :] for r in range(LR)]

    for copy in pre_copies:
        copy.wait()
    precondition(rh, 0, uh, 0, 0)
    pl.semaphore_wait(barrier, peers)
    halo_start(0, 0)
    put(zh, 0, ext_rows(0))
    precondition(tvec, 0, utv, 0, 1)
    halo_start(1, 1)
    put(tmv, 0, ext_rows(1))
    for n in range(NBLK):
        stiff_copy(n).wait()
    halo_finish(0, 0)
    stiffness(0, nvec)
    put(wh, 0, rows(nvec, 0))
    halo_finish(1, 1)
    stiffness(1, atv)
    halo_sent(0)
    halo_sent(1)

    def forward(i, carry):
        rho_old, gamma_old, c_old = carry[:3]
        z, w, res, t = rows(zh, i), rows(wh, i), rows(rh, i), rows(tvec, 0)
        q_old, s_old = rows(qh, i), rows(sh, i)
        sum_start(
            i,
            (
                (res, z), (z, w), (z, q_old), (t, z),
                (t, s_old), (w, s_old), (q_old, s_old),
            ),
        )
        precondition(wh, i * VEC, hvec, 0, 0)
        halo_start(2 + i, 0)
        at = factor_row(me, i, 0)
        put_at(fl, at, rows(uh, i))
        at = factor_row(me, i, 1)
        put_at(fr, at, rows(rh, i))
        factor_send(fl, 1, i, 0)
        factor_send(fr, 0, i, 1)
        halo_finish(2 + i, 0)
        stiffness(0, nvec)
        halo_sent(2 + i)
        tot = sum_finish(i)
        val = [[tot[r][d : d + 1, :] for r in range(LR)] for d in range(7)]
        rho, za, zq, tz = val[:4]
        first = jnp.broadcast_to(jnp.where(i == 0, 1, 0), (1, LANES)) > 0
        beta = [jnp.where(first, 0.0, a / b) for a, b in zip(rho, rho_old)]
        gamma = [
            za[r] + beta[r] * (2.0 * zq[r] + beta[r] * gamma_old[r]) for r in range(LR)
        ]
        c = axpy(tz, beta, c_old)
        alpha = [a / b for a, b in zip(rho, gamma)]
        minus = [-a for a in alpha]
        for kind, v in enumerate((alpha, gamma, rho, beta, c, zq)):
            keep(kind, i, v)
        p = axpy(rows(zh, i), beta, rows(ph, i))
        put(ph, i + 1, p)
        put(xv, 0, axpy(rows(xv, 0), alpha, p))
        q = axpy(rows(wh, i), beta, rows(qh, i))
        put(qh, i + 1, q)
        put(rh, i + 1, axpy(rows(rh, i), minus, q))
        s = axpy(ext_rows(0), beta, rows(sh, i))
        put(sh, i + 1, s)
        put(zh, i + 1, axpy(rows(zh, i), minus, s))
        y = axpy(rows(nvec, 0), beta, rows(yv, 0))
        put(yv, 0, y)
        put(wh, i + 1, axpy(rows(wh, i), minus, y))
        k = axpy(rows(hvec, 0), beta, rows(kv, 0))
        put(kv, 0, k)
        put(uh, i + 1, axpy(rows(uh, i), minus, k))
        return (
            tuple(rho), tuple(gamma), tuple(c),
            tuple(val[4]), tuple(val[5]), tuple(val[6]),
        )

    none = (jnp.zeros((1, LANES), jnp.float32),) * LR
    one = (jnp.ones((1, LANES), jnp.float32),) * LR
    last = lax.fori_loop(0, ITERS, forward, (one, none, none, none, none, none))
    gamma3, c3, ts, ws, qs = last[1:]

    def adjoint(i, bb, e0, e1, norm_bar, pb, wp, mp, amp):
        ratio = [a / b for a, b in zip(bb, kept(2, i))]
        full = [a + b for a, b in zip(norm_bar, ratio)]
        twice = [2.0 * a for a in full]
        zq, beta = kept(5, i + 1), kept(3, i + 1)
        err = [e0[r] + twice[r] * zq[r] + e1[r] for r in range(LR)]
        put_at(fr, factor_row(me, i + 1, 0), axpy(pb, full, rows(rh, i + 1)))
        put_at(fl, factor_row(me, i + 1, 1), axpy(wp, full, rows(uh, i + 1)))
        factor_send(fr, 0, i + 1, 0)
        factor_send(fl, 1, i + 1, 1)
        rb = axpy([a + b for a, b in zip(rows(rbv, 0), mp)], twice, rows(zh, i + 1))
        put(rbv, 0, rb)
        arb = axpy([a + b for a, b in zip(rows(arbv, 0), amp)], twice, rows(wh, i + 1))
        put(arbv, 0, arb)
        alpha, gamma = kept(0, i), kept(1, i)
        step_bar = [a - b for a, b in zip(kept(4, i), err)]
        curv2 = [-2.0 * (s * a / g) for s, a, g in zip(step_bar, alpha, gamma)]
        norm_bar = [s / g - a * b for s, g, a, b in zip(step_bar, gamma, ratio, beta)]
        diff = [a - b for a, b in zip(rows(tvec, 0), arb)]
        pb = axpy(axpy(scale(beta, pb), alpha, diff), curv2, rows(qh, i + 1))
        put(pbv, 0, pb)
        return tuple(norm_bar)

    alpha3, beta3, zq3 = kept(0, 3), kept(3, 3), kept(5, 3)
    gamma2, c2 = kept(1, 2), kept(4, 2)
    g2 = [-2.0 * (c * a / g) for c, a, g in zip(c3, alpha3, gamma3)]
    mix = lambda a, b: axpy(scale(alpha3, a), g2, b)
    bb = [
        alpha3[r] * c2[r] + g2[r] * (zq3[r] + beta3[r] * gamma2[r]) for r in range(LR)
    ]
    e1 = [alpha3[r] * ts[r] + g2[r] * (ws[r] + beta3[r] * qs[r]) for r in range(LR)]
    norm_bar = adjoint(
        2, bb, none, e1, [c / g for c, g in zip(c3, gamma3)],
        mix(rows(tvec, 0), rows(qh, 4)),
        mix(rows(utv, 0), rows(kv, 0)),
        mix(rows(tmv, 0), rows(sh, 4)),
        mix(rows(atv, 0), rows(yv, 0)),
    )

    def backward(it, norm_bar):
        i = 1 - it
        rd = ITERS + it
        pb = rows(pbv, 0)
        sum_start(
            rd,
            (
                (pb, rows(ph, i + 1)),
                (rows(rbv, 0), rows(qh, i + 1)),
                (pb, rows(sh, i + 1)),
            ),
        )
        precondition(pbv, 0, hvec, 0, 0)
        halo_start(2 + rd, 0)
        halo_finish(2 + rd, 0)
        stiffness(0, nvec)
        halo_sent(2 + rd)
        tot = sum_finish(rd)
        bb, e0, e1 = [[tot[r][d : d + 1, :] for r in range(LR)] for d in range(3)]
        return adjoint(
            i, bb, e0, e1, norm_bar,
            rows(pbv, 0), rows(hvec, 0), ext_rows(0), rows(nvec, 0),
        )

    norm_bar = lax.fori_loop(0, 2, backward, norm_bar)

    zeta = factor_row(me, 0, 0)
    put_at(fr, zeta, axpy(rows(pbv, 0), norm_bar, rows(rh, 0)))
    factor_send(fr, 0, 0, 0)
    precondition(fr, zeta, fl, factor_row(me, 0, 1), None)
    factor_send(fl, 1, 0, 1)

    for r in range(LR):
        parts = [xv[pl.ds(r * NBLK + j, 12, stride=4), :] for j in range(4)]
        for i, chunk in enumerate(rows_to_chunks(parts, lane12)):
            flat[0, pl.ds(2 * i + r, 12, stride=6), :] = chunk
    for c in range(ROWS // LR):
        sol_ref[:, pl.ds(c * LANES, LANES)] = flat[0, pl.ds(LR * c, LR), :]

    def factors_wait(j, _):
        for left, buf in ((1, fl), (0, fr)):
            for kind in range(2):
                for d in range(1, nrhs):
                    src = lax.rem(me + d, nrhs)
                    factor_copy(buf, left, j, kind, d, src, src).wait_recv()
                    factor_copy(buf, left, j, kind, d, me, src).wait_send()
        return 0

    lax.fori_loop(0, ITERS, factors_wait, 0)

    depth = nrhs * ITERS * 2 * LR
    lane24 = lax.broadcasted_iota(jnp.int32, (24, LANES), 1)

    def grads(t, _):
        for s in range(8):
            n = t * 8 + s
            lh, ll = halves(fl[pl.ds(n, depth, stride=NBLK), :])
            rhi, rlo = halves(fr[pl.ds(n, depth, stride=NBLK), :])
            gb[s] = lax.dot_general(
                jnp.concatenate([lh, lh, ll], axis=0),
                jnp.concatenate([rhi, rlo, rhi], axis=0),
                (((0,), (0,)), ((), ())),
                preferred_element_type=jnp.float32,
            )
            parts = [gb[s, pl.ds(j, 24, stride=4), :] for j in range(4)]
            for i, chunk in enumerate(rows_to_chunks(parts, lane24)):
                go[pl.ds(t * (CHUNKS * 8) + i * 8 + s, 24, stride=24), :] = chunk
        return 0

    lax.fori_loop(0, TILES, grads, 0)


def shards(nsub, nrhs, stiffness, precond, rhs_vec, cotangent, col_index, send_rows, counts):
    stiff = stiffness.reshape(NBLK, K, CHUNKS, LANES).transpose(0, 2, 1, 3)
    pre = precond.reshape(TILES, 8, CHUNKS, LANES).transpose(0, 2, 1, 3)
    f32 = jnp.float32
    vmem = pl.BlockSpec(memory_space=pltpu.VMEM)
    hbm = pl.BlockSpec(memory_space=pltpu.HBM)

    def vec(count=1):
        return pltpu.VMEM((count * VEC, LANES), f32)

    dma = pltpu.SemaphoreType.DMA
    factors = nrhs * ITERS * 2 * VEC
    sol, grad = pl.pallas_call(
        functools.partial(kernel, nsub, nrhs),
        out_shape=(
            jax.ShapeDtypeStruct((LR, NBLK * BS), f32),
            jax.ShapeDtypeStruct((TILES * CHUNKS * 8, LANES), f32),
        ),
        in_specs=[hbm, hbm, hbm, vmem, vmem, hbm, hbm],
        out_specs=(vmem, vmem),
        scratch_shapes=[
            pltpu.SMEM((K, NBLK), jnp.int32),
            pltpu.SMEM((1, 2 * IF), jnp.int32),
            pltpu.SMEM((1,), jnp.int32),
            pltpu.VMEM((2, ROWS, LANES), f32),
            pltpu.VMEM((CHUNKS, K, NBLK, LANES), f32),
            pltpu.VMEM((CHUNKS, NBLK, LANES), f32),
            pltpu.VMEM((2, LR * EXT, LANES), f32),
            vec(K - 1),
        ]
        + [vec() for _ in range(12)]
        + [vec(ITERS + 1) for _ in range(7)]
        + [
            pltpu.VMEM((LR * 6 * ITERS, LANES), f32),
            pltpu.VMEM((HALOS, 2, LR * 8, LANES), f32),
            pltpu.VMEM((HALOS, 2, LR * 8, LANES), f32),
            pltpu.VMEM((REDS * nsub, 1, LANES), f32),
            pltpu.VMEM((factors, LANES), f32),
            pltpu.VMEM((factors, LANES), f32),
            pltpu.VMEM((8, LANES, LANES), f32),
            dma((NBLK + TILES,)),
            dma((3,)),
            dma((HALOS, 2)),
            dma((HALOS, 2)),
            dma((REDS,)),
            dma((REDS,)),
            dma((ITERS * 16,)),
            dma((ITERS * 16,)),
        ],
        compiler_params=pltpu.CompilerParams(
            collective_id=0, has_side_effects=True, vmem_limit_bytes=48 * 1024 * 1024
        ),
        name="cg_adjoint",
    )(col_index.T, send_rows, counts, rhs_vec, cotangent, stiff, pre)
    grad = grad.reshape(TILES, CHUNKS, 8, LANES).transpose(0, 2, 1, 3)
    return sol, grad.reshape(NBLK, BS * BS)


def solution(mesh):
    in_specs = (
        P("sub", None, None),
        P("sub", None),
        P("rhs", "sub"),
        P("rhs", "sub"),
        P("sub", None),
        P("sub", None),
        P("sub"),
    )
    out_specs = (P("rhs", "sub"), P("sub", None))
    body = functools.partial(shards, mesh.shape["sub"], mesh.shape["rhs"])
    return jax.shard_map(body, mesh=mesh, in_specs=in_specs, out_specs=out_specs, check_vma=False)
```

```python
import functools

import jax
import jax.numpy as jnp
from jax import lax
from jax.experimental import pallas as pl
from jax.experimental.pallas import tpu as pltpu
from jax.sharding import PartitionSpec as P

BS = 96
K = 4
NBLK = 48
IF = 6
ITERS = 4
LR = 2
LANES = 128
TILES = NBLK // 8
CHUNKS = BS * BS // LANES
VEC = LR * NBLK
ROWS = LR * BS * NBLK // LANES
GROUPS = CHUNKS // 3
HALOS = 8
REDS = 6
EXT = 56
RIM = 24
MESH = pl.DeviceIdType.MESH


def lane_iota():
    return lax.broadcasted_iota(jnp.int32, (8, LANES), 1)


def patterns(x, lane):
    far = pltpu.roll(x, 96, 1)
    mid = pltpu.roll(x, 64, 1)
    near = pltpu.roll(x, 32, 1)
    return (
        jnp.where(lane < 96, x, far),
        jnp.where(lane < 64, far, mid),
        jnp.where(lane < 32, mid, near),
    )


def row_parts(p, lane):
    zero = jnp.zeros_like(p[0])
    return (
        jnp.where(lane < 96, p[0], zero),
        jnp.where(lane < 64, p[1], jnp.where(lane >= 96, p[0], zero)),
        jnp.where(lane >= 64, p[1], jnp.where(lane < 32, p[2], zero)),
        jnp.where(lane >= 32, p[2], zero),
    )


def rows_to_chunks(r, lane):
    far = pltpu.roll(r[1], 96, 1)
    mid = pltpu.roll(r[2], 64, 1)
    return (
        jnp.where(lane < 96, r[0], far),
        jnp.where(lane < 64, far, mid),
        jnp.where(lane < 32, mid, pltpu.roll(r[3], 32, 1)),
    )


def chunks_to_rows(c, lane):
    zero = jnp.zeros_like(c[0])
    rows = (
        c[0],
        pltpu.roll(jnp.where(lane >= 96, c[0], c[1]), 32, 1),
        pltpu.roll(jnp.where(lane >= 64, c[1], c[2]), 64, 1),
        pltpu.roll(c[2], 96, 1),
    )
    return [jnp.where(lane < 96, r, zero) for r in rows]


def kernel(
    nsub, nrhs,
    col_hbm, send_hbm, count_hbm, rhs_ref, cot_ref, stiff_hbm, pre_hbm,
    sol_ref, go,
    colx, rimx, sendx, countx, flat, blocks, faces, weights, ext, gat, rim, rimg,
    nvec, hvec, tvec, tmv, utv, atv, yv, kv, xv, pbv, rbv, arbv,
    ph, qh, sh, zh, wh, rh, uh, scr, hsend, hrecv, rbuf, fl, fr, gb,
    load_sem, small_sem, hs_sem, hr_sem, rs_sem, rr_sem, fs_sem, fr_sem,
):
    sub = lax.axis_index("sub")
    me = lax.axis_index("rhs")
    lane = lane_iota()
    f32, bf16 = jnp.float32, jnp.bfloat16

    small = [
        pltpu.make_async_copy(col_hbm, colx, small_sem.at[0]),
        pltpu.make_async_copy(send_hbm, sendx, small_sem.at[1]),
        pltpu.make_async_copy(count_hbm, countx, small_sem.at[2]),
    ]
    pre_copies = [
        pltpu.make_async_copy(
            pre_hbm.at[t], weights.at[:, pl.ds(8 * t, 8), :], load_sem.at[NBLK + t]
        )
        for t in range(TILES)
    ]
    for copy in small + pre_copies:
        copy.start()

    def stiff_copy(n):
        return pltpu.make_async_copy(stiff_hbm.at[n], blocks.at[:, :, n, :], load_sem.at[n])

    for n in range(NBLK):
        stiff_copy(n).start()

    barrier = pltpu.get_barrier_semaphore()

    def greet(d, _):
        pl.semaphore_signal(
            barrier, inc=1, device_id={"sub": lax.rem(sub + d, nsub)}, device_id_type=MESH
        )
        return 0

    lax.fori_loop(1, nsub, greet, 0)
    for d in range(1, nrhs):
        pl.semaphore_signal(
            barrier, inc=1, device_id={"rhs": lax.rem(me + d, nrhs)}, device_id_type=MESH
        )
    peers = nsub - 1 + nrhs - 1
    before = lax.rem(sub + nsub - 1, nsub)
    after = lax.rem(sub + 1, nsub)

    hsend[...] = jnp.zeros_like(hsend)
    for ref in (ph, qh, sh):
        ref[pl.ds(0, VEC), :] = jnp.zeros((VEC, LANES), f32)
    for ref in (yv, kv, xv, rbv, arbv):
        ref[...] = jnp.zeros_like(ref)
    for copy in small:
        copy.wait()
    for q in range(2 * IF):
        for k in range(1, K):
            c = colx[k, sendx[0, q]]
            rimx[k, q] = jnp.where(
                c < IF, c, jnp.where(c < IF + NBLK, 16, c + 8 - IF - NBLK)
            )
    for n in range(NBLK):
        for k in range(1, K):
            c = colx[k, n] - IF
            colx[k, n] = jnp.where((c >= 0) & (c < NBLK), c, NBLK)
    ext[...] = jnp.zeros_like(ext)
    rim[...] = jnp.zeros_like(rim)
    rimg[...] = jnp.zeros_like(rimg)

    def clear(c, _):
        faces[c] = jnp.zeros((K - 1, 16, LANES), f32)
        return 0

    lax.fori_loop(0, CHUNKS, clear, 0)

    lane12 = lax.broadcasted_iota(jnp.int32, (12, LANES), 1)
    row12 = lax.broadcasted_iota(jnp.int32, (12, LANES), 0)
    live = countx[0]
    for c in range(ROWS // LR):
        flat[0, pl.ds(LR * c, LR), :] = rhs_ref[:, pl.ds(c * LANES, LANES)]
        flat[1, pl.ds(LR * c, LR), :] = cot_ref[:, pl.ds(c * LANES, LANES)]
    for r in range(LR):
        chunks = [flat[0, pl.ds(2 * i + r, 12, stride=6), :] for i in range(3)]
        for j, row in enumerate(chunks_to_rows(chunks, lane12)):
            row = jnp.where(row12 * 4 + j < live, row, jnp.zeros_like(row))
            rh[pl.ds(r * NBLK + j, 12, stride=4), :] = row
        chunks = [flat[1, pl.ds(2 * i + r, 12, stride=6), :] for i in range(3)]
        for j, row in enumerate(chunks_to_rows(chunks, lane12)):
            tvec[pl.ds(r * NBLK + j, 12, stride=4), :] = row

    def halves(v):
        hi = v.astype(bf16)
        return hi, (v - hi.astype(f32)).astype(bf16)

    def row_sums(v):
        return [
            jnp.broadcast_to(jnp.sum(p, axis=1, keepdims=True), (8, LANES))
            for p in row_parts(v, lane)
        ]

    def precondition(src, base, dst, dst_base, slot, rd=None):
        full = slot is not None

        def pair(s, _):
            if rd is not None:
                for q in range((nsub - 1) // 3):
                    sum_copy(rd, s * ((nsub - 1) // 3) + q).start()
            tiles = (2 * s, 2 * s + 1)
            at = [pl.multiple_of(8 * t, 8) for t in tiles]
            items = [(b, r) for b in range(2) for r in range(LR)]
            x = {
                (b, r): src[pl.ds(pl.multiple_of(base + r * NBLK + at[b], 8), 8), :]
                for b, r in items
            }
            pat = {m: patterns(x[m], lane) for m in items}
            zero = jnp.zeros((8, LANES), f32)
            proj = {m: zero for m in items}
            acc = {m: [zero] * 3 for m in items}
            for g in range(GROUPS):
                for b in range(2):
                    w = [weights[3 * g + i, pl.ds(at[b], 8), :] for i in range(3)]
                    for r in range(LR):
                        m = (b, r)
                        sums = row_sums([w[i] * pat[m][i] for i in range(3)])
                        for j in range(4):
                            proj[m] = jnp.where(lane == 4 * g + j, sums[j], proj[m])
                        if full:
                            acc[m][0] += w[0] * jnp.where(lane < 96, sums[0], sums[1])
                            acc[m][1] += w[1] * jnp.where(lane < 64, sums[1], sums[2])
                            acc[m][2] += w[2] * jnp.where(lane < 32, sums[2], sums[3])
            for b, r in items:
                dst[pl.ds(pl.multiple_of(dst_base + r * NBLK + at[b], 8), 8), :] = proj[b, r]
                if full:
                    a = acc[b, r]
                    total = (
                        a[0]
                        + pltpu.roll(jnp.where(lane >= 96, a[0], a[1]), 32, 1)
                        + pltpu.roll(jnp.where(lane >= 64, a[1], a[2]), 64, 1)
                        + pltpu.roll(a[2], 96, 1)
                    )
                    ext[slot, pl.ds(pl.multiple_of(r * EXT + at[b], 8), 8), :] = x[
                        b, r
                    ] + jnp.where(lane < 96, total, zero)
            return 0

        lax.fori_loop(0, TILES // 2, pair, 0)

    def halo_copies(h):
        return (
            pltpu.make_async_remote_copy(
                src_ref=hsend.at[h, 0], dst_ref=hrecv.at[h, 1],
                send_sem=hs_sem.at[h, 0], recv_sem=hr_sem.at[h, 1],
                device_id={"sub": before}, device_id_type=MESH,
            ),
            pltpu.make_async_remote_copy(
                src_ref=hsend.at[h, 1], dst_ref=hrecv.at[h, 0],
                send_sem=hs_sem.at[h, 1], recv_sem=hr_sem.at[h, 0],
                device_id={"sub": after}, device_id_type=MESH,
            ),
        )

    def halo_start(h, slot):
        for side in range(2):
            for j in range(IF):
                idx = sendx[0, side * IF + j]
                for r in range(LR):
                    hsend[h, side, pl.ds(r * 8 + j, 1), :] = ext[slot, pl.ds(r * EXT + idx, 1), :]
        for copy in halo_copies(h):
            copy.start()

    def halo_finish(h, dst):
        for copy in halo_copies(h):
            copy.wait_recv()
        for side in range(2):
            edge = jnp.where(sub == (0 if side == 0 else nsub - 1), 0, 1)
            inside = jnp.broadcast_to(edge, (8, LANES)) > 0
            for r in range(LR):
                v = hrecv[h, side, pl.ds(r * 8, 8), :]
                rim[pl.ds(r * RIM + 8 * side, 8), :] = jnp.where(inside, v, jnp.zeros_like(v))
        for q in range(2 * IF):
            for k in range(1, K):
                c = rimx[k, q]
                for r in range(LR):
                    rimg[pl.ds(((k - 1) * LR + r) * 16 + q, 1), :] = rim[pl.ds(r * RIM + c, 1), :]
        out = {}
        for t in range(2):
            pat = [
                [
                    patterns(rimg[pl.ds(((k - 1) * LR + r) * 16 + 8 * t, 8), :], lane)
                    for k in range(1, K)
                ]
                for r in range(LR)
            ]
            acc = [jnp.zeros((8, LANES), f32)] * LR
            for g in range(GROUPS):
                prod = [[None] * 3 for _ in range(LR)]
                for i in range(3):
                    a = [faces[3 * g + i, k, pl.ds(8 * t, 8), :] for k in range(K - 1)]
                    for r in range(LR):
                        prod[r][i] = (a[0] * pat[r][0][i] + a[1] * pat[r][1][i]) + (
                            a[2] * pat[r][2][i]
                        )
                for r in range(LR):
                    for j, v in enumerate(row_sums(prod[r])):
                        acc[r] = jnp.where(lane == 4 * g + j, v, acc[r])
            for r in range(LR):
                out[t, r] = acc[r]
        block = lax.broadcasted_iota(jnp.int32, (NBLK, LANES), 0)
        total = [dst[pl.ds(r * NBLK, NBLK), :] for r in range(LR)]
        for q in range(2 * IF):
            hit = block == sendx[0, q]
            for r in range(LR):
                row = jnp.broadcast_to(out[q // 8, r][q % 8 : q % 8 + 1], (NBLK, LANES))
                total[r] = total[r] + jnp.where(hit, row, jnp.zeros_like(row))
        for r in range(LR):
            dst[pl.ds(r * NBLK, NBLK), :] = total[r]

    def halo_sent(h):
        for copy in halo_copies(h):
            copy.wait_send()

    def stiffness(slot, dst):
        def gather(s, _):
            for q in range(4):
                n = s * 4 + q
                for k in range(1, K):
                    c = colx[k, n]
                    for r in range(LR):
                        gat[pl.ds(((k - 1) * LR + r) * NBLK + n, 1), :] = ext[
                            slot, pl.ds(r * EXT + c, 1), :
                        ]
            return 0

        lax.fori_loop(0, NBLK // 4, gather, 0)

        def tile(t, _):
            at = pl.multiple_of(8 * t, 8)
            pat = []
            for r in range(LR):
                own = ext[slot, pl.ds(pl.multiple_of(r * EXT + 8 * t, 8), 8), :]
                rest = [
                    gat[pl.ds(pl.multiple_of(((k - 1) * LR + r) * NBLK + 8 * t, 8), 8), :]
                    for k in range(1, K)
                ]
                pat.append([patterns(v, lane) for v in [own] + rest])

            out = [jnp.zeros((8, LANES), f32)] * LR
            for g in range(GROUPS):
                prod = [[None] * 3 for _ in range(LR)]
                for i in range(3):
                    a = [blocks[3 * g + i, k, pl.ds(at, 8), :] for k in range(K)]
                    for r in range(LR):
                        prod[r][i] = (a[0] * pat[r][0][i] + a[1] * pat[r][1][i]) + (
                            a[2] * pat[r][2][i] + a[3] * pat[r][3][i]
                        )
                for r in range(LR):
                    for j, v in enumerate(row_sums(prod[r])):
                        out[r] = jnp.where(lane == 4 * g + j, v, out[r])
            for r in range(LR):
                dst[pl.ds(pl.multiple_of(r * NBLK + 8 * t, 8), 8), :] = out[r]
            return 0

        lax.fori_loop(0, TILES, tile, 0)

    def sum_copy(rd, m):
        d = nsub // 2 + lax.div(m + 1, 2) * (2 * lax.rem(m, 2) - 1)
        at = rd * nsub + sub
        return pltpu.make_async_remote_copy(
            src_ref=rbuf.at[at], dst_ref=rbuf.at[at],
            send_sem=rs_sem.at[rd], recv_sem=rr_sem.at[rd],
            device_id={"sub": lax.rem(sub + d, nsub)}, device_id_type=MESH,
        )

    srow = lax.broadcasted_iota(jnp.int32, (8, LANES), 0)

    def sum_local(rd, pairs):
        payload = jnp.zeros((8, LANES), f32)
        for r in range(LR):
            tile = jnp.zeros((8, LANES), f32)
            for d, (a, b) in enumerate(pairs):
                row = jnp.sum(a[r] * b[r], axis=0, keepdims=True)
                tile = jnp.where(srow == d, jnp.broadcast_to(row, (8, LANES)), tile)
            tot = jnp.broadcast_to(jnp.sum(tile, axis=1, keepdims=True), (8, LANES))
            payload = jnp.where(lane == srow + 64 * r, tot, payload)
        rbuf[rd * nsub + sub] = jnp.sum(payload, axis=0, keepdims=True)

    def sum_finish(rd):
        span = rbuf.at[pl.ds(rd * nsub, nsub - 1)]
        pltpu.make_async_copy(span, span, rr_sem.at[rd]).wait()
        parts = [jnp.zeros((1, LANES), f32)] * 4
        for s in range(nsub):
            parts[s % 4] = parts[s % 4] + rbuf[rd * nsub + s]
        row = jnp.broadcast_to((parts[0] + parts[1]) + (parts[2] + parts[3]), (8, LANES))
        pltpu.make_async_copy(span, span, rs_sem.at[rd]).wait()
        return [
            jnp.broadcast_to(
                jnp.sum(
                    jnp.where(lane == srow + 64 * r, row, jnp.zeros_like(row)),
                    axis=1, keepdims=True,
                ),
                (8, LANES),
            )
            for r in range(LR)
        ]

    def factor_row(src, j, kind):
        return pl.multiple_of(((src * ITERS + j) * 2 + kind) * VEC, 8)

    def factor_copy(buf, left, j, kind, d, src, target):
        at = factor_row(src, j, kind)
        piece = (j * 2 + left) * 2 + kind
        return pltpu.make_async_remote_copy(
            src_ref=buf.at[pl.ds(at, VEC), :], dst_ref=buf.at[pl.ds(at, VEC), :],
            send_sem=fs_sem.at[piece * 4 + d], recv_sem=fr_sem.at[piece * 4 + src],
            device_id={"rhs": target}, device_id_type=MESH,
        )

    def factor_send(buf, left, j, kind):
        for d in range(1, nrhs):
            factor_copy(buf, left, j, kind, d, me, lax.rem(me + d, nrhs)).start()

    def rows(ref, i):
        return [
            ref[pl.ds(pl.multiple_of(i * VEC + r * NBLK, 8), NBLK), :] for r in range(LR)
        ]

    def put(ref, i, v):
        for r in range(LR):
            ref[pl.ds(pl.multiple_of(i * VEC + r * NBLK, 8), NBLK), :] = v[r]

    def put_at(ref, base, v):
        for r in range(LR):
            ref[pl.ds(pl.multiple_of(base + r * NBLK, 8), NBLK), :] = v[r]

    def ext_rows(slot):
        return [ext[slot, pl.ds(r * EXT, NBLK), :] for r in range(LR)]

    def axpy(x, s, y):
        return [a + c * b for a, c, b in zip(x, s, y)]

    def scale(s, y):
        return [c * b for c, b in zip(s, y)]

    def keep(kind, i, v):
        for r in range(LR):
            scr[pl.ds((r * 6 + kind) * ITERS + i, 1), :] = v[r]

    def kept(kind, i):
        return [scr[pl.ds((r * 6 + kind) * ITERS + i, 1), :] for r in range(LR)]

    for copy in pre_copies:
        copy.wait()
    precondition(rh, 0, uh, 0, 0)
    pl.semaphore_wait(barrier, peers)
    halo_start(0, 0)
    put(zh, 0, ext_rows(0))
    precondition(tvec, 0, utv, 0, 1)
    halo_start(1, 1)
    put(tmv, 0, ext_rows(1))
    for n in range(NBLK):
        stiff_copy(n).wait()

    def face(c, _):
        for k in range(1, K):
            for q in range(2 * IF):
                faces[c, k - 1, pl.ds(q, 1), :] = blocks[c, k, pl.ds(sendx[0, q], 1), :]
        return 0

    lax.fori_loop(0, CHUNKS, face, 0)
    stiffness(0, nvec)
    halo_finish(0, nvec)
    put(wh, 0, rows(nvec, 0))
    stiffness(1, atv)
    halo_finish(1, atv)
    halo_sent(0)
    halo_sent(1)

    def forward(i, carry):
        rho_old, gamma_old, c_old = carry[:3]
        z, w, res, t = rows(zh, i), rows(wh, i), rows(rh, i), rows(tvec, 0)
        q_old, s_old = rows(qh, i), rows(sh, i)
        sum_local(
            i,
            (
                (res, z), (z, w), (z, q_old), (t, z),
                (t, s_old), (w, s_old), (q_old, s_old),
            ),
        )
        precondition(wh, i * VEC, hvec, 0, 0, i)
        halo_start(2 + i, 0)
        at = factor_row(me, i, 0)
        put_at(fl, at, rows(uh, i))
        at = factor_row(me, i, 1)
        put_at(fr, at, rows(rh, i))
        factor_send(fl, 1, i, 0)
        factor_send(fr, 0, i, 1)
        stiffness(0, nvec)
        halo_finish(2 + i, nvec)
        halo_sent(2 + i)
        tot = sum_finish(i)
        val = [[tot[r][d : d + 1, :] for r in range(LR)] for d in range(7)]
        rho, za, zq, tz = val[:4]
        first = jnp.broadcast_to(jnp.where(i == 0, 1, 0), (1, LANES)) > 0
        beta = [jnp.where(first, 0.0, a / b) for a, b in zip(rho, rho_old)]
        gamma = [
            za[r] + beta[r] * (2.0 * zq[r] + beta[r] * gamma_old[r]) for r in range(LR)
        ]
        c = axpy(tz, beta, c_old)
        alpha = [a / b for a, b in zip(rho, gamma)]
        minus = [-a for a in alpha]
        for kind, v in enumerate((alpha, gamma, rho, beta, c, zq)):
            keep(kind, i, v)
        p = axpy(rows(zh, i), beta, rows(ph, i))
        put(ph, i + 1, p)
        put(xv, 0, axpy(rows(xv, 0), alpha, p))
        q = axpy(rows(wh, i), beta, rows(qh, i))
        put(qh, i + 1, q)
        put(rh, i + 1, axpy(rows(rh, i), minus, q))
        s = axpy(ext_rows(0), beta, rows(sh, i))
        put(sh, i + 1, s)
        put(zh, i + 1, axpy(rows(zh, i), minus, s))
        y = axpy(rows(nvec, 0), beta, rows(yv, 0))
        put(yv, 0, y)
        put(wh, i + 1, axpy(rows(wh, i), minus, y))
        k = axpy(rows(hvec, 0), beta, rows(kv, 0))
        put(kv, 0, k)
        put(uh, i + 1, axpy(rows(uh, i), minus, k))
        return (
            tuple(rho), tuple(gamma), tuple(c),
            tuple(val[4]), tuple(val[5]), tuple(val[6]),
        )

    none = (jnp.zeros((1, LANES), jnp.float32),) * LR
    one = (jnp.ones((1, LANES), jnp.float32),) * LR
    last = lax.fori_loop(0, ITERS, forward, (one, none, none, none, none, none))
    gamma3, c3, ts, ws, qs = last[1:]

    def adjoint(i, bb, e0, e1, norm_bar, pb, wp, mp, amp):
        ratio = [a / b for a, b in zip(bb, kept(2, i))]
        full = [a + b for a, b in zip(norm_bar, ratio)]
        twice = [2.0 * a for a in full]
        zq, beta = kept(5, i + 1), kept(3, i + 1)
        err = [e0[r] + twice[r] * zq[r] + e1[r] for r in range(LR)]
        put_at(fr, factor_row(me, i + 1, 0), axpy(pb, full, rows(rh, i + 1)))
        put_at(fl, factor_row(me, i + 1, 1), axpy(wp, full, rows(uh, i + 1)))
        factor_send(fr, 0, i + 1, 0)
        factor_send(fl, 1, i + 1, 1)
        rb = axpy([a + b for a, b in zip(rows(rbv, 0), mp)], twice, rows(zh, i + 1))
        put(rbv, 0, rb)
        arb = axpy([a + b for a, b in zip(rows(arbv, 0), amp)], twice, rows(wh, i + 1))
        put(arbv, 0, arb)
        alpha, gamma = kept(0, i), kept(1, i)
        step_bar = [a - b for a, b in zip(kept(4, i), err)]
        curv2 = [-2.0 * (s * a / g) for s, a, g in zip(step_bar, alpha, gamma)]
        norm_bar = [s / g - a * b for s, g, a, b in zip(step_bar, gamma, ratio, beta)]
        diff = [a - b for a, b in zip(rows(tvec, 0), arb)]
        pb = axpy(axpy(scale(beta, pb), alpha, diff), curv2, rows(qh, i + 1))
        put(pbv, 0, pb)
        return tuple(norm_bar)

    alpha3, beta3, zq3 = kept(0, 3), kept(3, 3), kept(5, 3)
    gamma2, c2 = kept(1, 2), kept(4, 2)
    g2 = [-2.0 * (c * a / g) for c, a, g in zip(c3, alpha3, gamma3)]
    mix = lambda a, b: axpy(scale(alpha3, a), g2, b)
    bb = [
        alpha3[r] * c2[r] + g2[r] * (zq3[r] + beta3[r] * gamma2[r]) for r in range(LR)
    ]
    e1 = [alpha3[r] * ts[r] + g2[r] * (ws[r] + beta3[r] * qs[r]) for r in range(LR)]
    norm_bar = adjoint(
        2, bb, none, e1, [c / g for c, g in zip(c3, gamma3)],
        mix(rows(tvec, 0), rows(qh, 4)),
        mix(rows(utv, 0), rows(kv, 0)),
        mix(rows(tmv, 0), rows(sh, 4)),
        mix(rows(atv, 0), rows(yv, 0)),
    )

    def backward(it, norm_bar):
        i = 1 - it
        rd = ITERS + it
        pb = rows(pbv, 0)
        sum_local(
            rd,
            (
                (pb, rows(ph, i + 1)),
                (rows(rbv, 0), rows(qh, i + 1)),
                (pb, rows(sh, i + 1)),
            ),
        )
        precondition(pbv, 0, hvec, 0, 0, rd)
        halo_start(2 + rd, 0)
        stiffness(0, nvec)
        halo_finish(2 + rd, nvec)
        halo_sent(2 + rd)
        tot = sum_finish(rd)
        bb, e0, e1 = [[tot[r][d : d + 1, :] for r in range(LR)] for d in range(3)]
        return adjoint(
            i, bb, e0, e1, norm_bar,
            rows(pbv, 0), rows(hvec, 0), ext_rows(0), rows(nvec, 0),
        )

    norm_bar = lax.fori_loop(0, 2, backward, norm_bar)

    zeta = factor_row(me, 0, 0)
    put_at(fr, zeta, axpy(rows(pbv, 0), norm_bar, rows(rh, 0)))
    factor_send(fr, 0, 0, 0)
    precondition(fr, zeta, fl, factor_row(me, 0, 1), None)
    factor_send(fl, 1, 0, 1)

    for r in range(LR):
        parts = [xv[pl.ds(r * NBLK + j, 12, stride=4), :] for j in range(4)]
        for i, chunk in enumerate(rows_to_chunks(parts, lane12)):
            flat[0, pl.ds(2 * i + r, 12, stride=6), :] = chunk
    for c in range(ROWS // LR):
        sol_ref[:, pl.ds(c * LANES, LANES)] = flat[0, pl.ds(LR * c, LR), :]

    def factors_wait(j, _):
        for left, buf in ((1, fl), (0, fr)):
            for kind in range(2):
                for d in range(1, nrhs):
                    src = lax.rem(me + d, nrhs)
                    factor_copy(buf, left, j, kind, d, src, src).wait_recv()
                    factor_copy(buf, left, j, kind, d, me, src).wait_send()
        return 0

    lax.fori_loop(0, ITERS, factors_wait, 0)

    depth = nrhs * ITERS * 2 * LR
    lane24 = lax.broadcasted_iota(jnp.int32, (24, LANES), 1)

    def grads(t, _):
        for s in range(8):
            n = t * 8 + s
            lh, ll = halves(fl[pl.ds(n, depth, stride=NBLK), :])
            rhi, rlo = halves(fr[pl.ds(n, depth, stride=NBLK), :])
            gb[s] = lax.dot_general(
                jnp.concatenate([lh, lh, ll], axis=0),
                jnp.concatenate([rhi, rlo, rhi], axis=0),
                (((0,), (0,)), ((), ())),
                preferred_element_type=jnp.float32,
            )
            parts = [gb[s, pl.ds(j, 24, stride=4), :] for j in range(4)]
            for i, chunk in enumerate(rows_to_chunks(parts, lane24)):
                go[pl.ds(t * (CHUNKS * 8) + i * 8 + s, 24, stride=24), :] = chunk
        return 0

    lax.fori_loop(0, TILES, grads, 0)


def shards(nsub, nrhs, stiffness, precond, rhs_vec, cotangent, col_index, send_rows, counts):
    stiff = stiffness.reshape(NBLK, K, CHUNKS, LANES).transpose(0, 2, 1, 3)
    pre = precond.reshape(TILES, 8, CHUNKS, LANES).transpose(0, 2, 1, 3)
    f32 = jnp.float32
    vmem = pl.BlockSpec(memory_space=pltpu.VMEM)
    hbm = pl.BlockSpec(memory_space=pltpu.HBM)

    def vec(count=1):
        return pltpu.VMEM((count * VEC, LANES), f32)

    dma = pltpu.SemaphoreType.DMA
    factors = nrhs * ITERS * 2 * VEC
    sol, grad = pl.pallas_call(
        functools.partial(kernel, nsub, nrhs),
        out_shape=(
            jax.ShapeDtypeStruct((LR, NBLK * BS), f32),
            jax.ShapeDtypeStruct((TILES * CHUNKS * 8, LANES), f32),
        ),
        in_specs=[hbm, hbm, hbm, vmem, vmem, hbm, hbm],
        out_specs=(vmem, vmem),
        scratch_shapes=[
            pltpu.SMEM((K, NBLK), jnp.int32),
            pltpu.SMEM((K, 2 * IF), jnp.int32),
            pltpu.SMEM((1, 2 * IF), jnp.int32),
            pltpu.SMEM((1,), jnp.int32),
            pltpu.VMEM((2, ROWS, LANES), f32),
            pltpu.VMEM((CHUNKS, K, NBLK, LANES), f32),
            pltpu.VMEM((CHUNKS, K - 1, 16, LANES), f32),
            pltpu.VMEM((CHUNKS, NBLK, LANES), f32),
            pltpu.VMEM((2, LR * EXT, LANES), f32),
            vec(K - 1),
            pltpu.VMEM((LR * RIM, LANES), f32),
            pltpu.VMEM(((K - 1) * LR * 16, LANES), f32),
        ]
        + [vec() for _ in range(12)]
        + [vec(ITERS + 1) for _ in range(7)]
        + [
            pltpu.VMEM((LR * 6 * ITERS, LANES), f32),
            pltpu.VMEM((HALOS, 2, LR * 8, LANES), f32),
            pltpu.VMEM((HALOS, 2, LR * 8, LANES), f32),
            pltpu.VMEM((REDS * nsub, 1, LANES), f32),
            pltpu.VMEM((factors, LANES), f32),
            pltpu.VMEM((factors, LANES), f32),
            pltpu.VMEM((8, LANES, LANES), f32),
            dma((NBLK + TILES,)),
            dma((3,)),
            dma((HALOS, 2)),
            dma((HALOS, 2)),
            dma((REDS,)),
            dma((REDS,)),
            dma((ITERS * 16,)),
            dma((ITERS * 16,)),
        ],
        compiler_params=pltpu.CompilerParams(
            collective_id=0, has_side_effects=True, vmem_limit_bytes=62 * 1024 * 1024
        ),
        name="cg_adjoint",
    )(col_index.T, send_rows, counts, rhs_vec, cotangent, stiff, pre)
    grad = grad.reshape(TILES, CHUNKS, 8, LANES).transpose(0, 2, 1, 3)
    return sol, grad.reshape(NBLK, BS * BS)


def solution(mesh):
    in_specs = (
        P("sub", None, None),
        P("sub", None),
        P("rhs", "sub"),
        P("rhs", "sub"),
        P("sub", None),
        P("sub", None),
        P("sub"),
    )
    out_specs = (P("rhs", "sub"), P("sub", None))
    body = functools.partial(shards, mesh.shape["sub"], mesh.shape["rhs"])
    return jax.shard_map(body, mesh=mesh, in_specs=in_specs, out_specs=out_specs, check_vma=False)
```

```python
import functools

import jax
import jax.numpy as jnp
from jax import lax
from jax.experimental import pallas as pl
from jax.experimental.pallas import tpu as pltpu
from jax.sharding import PartitionSpec as P

BS = 96
K = 4
NBLK = 48
IF = 6
ITERS = 4
LR = 2
LANES = 128
TILES = NBLK // 8
CHUNKS = BS * BS // LANES
VEC = LR * NBLK
ROWS = LR * BS * NBLK // LANES
GROUPS = CHUNKS // 3
HALOS = 8
REDS = 6
EXT = 56
RIM = 24
MESH = pl.DeviceIdType.MESH


def lane_iota():
    return lax.broadcasted_iota(jnp.int32, (8, LANES), 1)


def patterns(x, lane):
    far = pltpu.roll(x, 96, 1)
    mid = pltpu.roll(x, 64, 1)
    near = pltpu.roll(x, 32, 1)
    return (
        jnp.where(lane < 96, x, far),
        jnp.where(lane < 64, far, mid),
        jnp.where(lane < 32, mid, near),
    )


def row_parts(p, lane):
    zero = jnp.zeros_like(p[0])
    return (
        jnp.where(lane < 96, p[0], zero),
        jnp.where(lane < 64, p[1], jnp.where(lane >= 96, p[0], zero)),
        jnp.where(lane >= 64, p[1], jnp.where(lane < 32, p[2], zero)),
        jnp.where(lane >= 32, p[2], zero),
    )


def rows_to_chunks(r, lane):
    far = pltpu.roll(r[1], 96, 1)
    mid = pltpu.roll(r[2], 64, 1)
    return (
        jnp.where(lane < 96, r[0], far),
        jnp.where(lane < 64, far, mid),
        jnp.where(lane < 32, mid, pltpu.roll(r[3], 32, 1)),
    )


def chunks_to_rows(c, lane):
    zero = jnp.zeros_like(c[0])
    rows = (
        c[0],
        pltpu.roll(jnp.where(lane >= 96, c[0], c[1]), 32, 1),
        pltpu.roll(jnp.where(lane >= 64, c[1], c[2]), 64, 1),
        pltpu.roll(c[2], 96, 1),
    )
    return [jnp.where(lane < 96, r, zero) for r in rows]


def kernel(
    nsub, nrhs,
    col_hbm, send_hbm, count_hbm, rhs_ref, cot_ref, stiff_hbm, pre_hbm,
    sol_ref, go,
    colx, rimx, sendx, countx, flat, blocks, faces, weights, ext, gat, rim, rimg,
    nvec, hvec, tvec, tmv, utv, atv, yv, kv, xv, pbv, rbv, arbv,
    ph, qh, sh, zh, wh, rh, uh, scr, hsend, hrecv, rbuf, fl, fr, nf, gb,
    load_sem, small_sem, hs_sem, hr_sem, rs_sem, rr_sem, fs_sem, fr_sem, ns_sem, nr_sem,
):
    sub = lax.axis_index("sub")
    me = lax.axis_index("rhs")
    lane = lane_iota()
    f32, bf16 = jnp.float32, jnp.bfloat16

    small = [
        pltpu.make_async_copy(col_hbm, colx, small_sem.at[0]),
        pltpu.make_async_copy(send_hbm, sendx, small_sem.at[1]),
        pltpu.make_async_copy(count_hbm, countx, small_sem.at[2]),
    ]
    pre_copies = [
        pltpu.make_async_copy(
            pre_hbm.at[t], weights.at[:, pl.ds(8 * t, 8), :], load_sem.at[NBLK + t]
        )
        for t in range(TILES)
    ]
    for copy in small + pre_copies:
        copy.start()

    def stiff_copy(n):
        return pltpu.make_async_copy(stiff_hbm.at[n], blocks.at[:, :, n, :], load_sem.at[n])

    for n in range(NBLK):
        stiff_copy(n).start()

    barrier = pltpu.get_barrier_semaphore()

    def greet(d, _):
        pl.semaphore_signal(
            barrier, inc=1, device_id={"sub": lax.rem(sub + d, nsub)}, device_id_type=MESH
        )
        return 0

    lax.fori_loop(1, nsub, greet, 0)
    for d in range(1, nrhs):
        pl.semaphore_signal(
            barrier, inc=1, device_id={"rhs": lax.rem(me + d, nrhs)}, device_id_type=MESH
        )
    peers = nsub - 1 + nrhs - 1
    before = lax.rem(sub + nsub - 1, nsub)
    after = lax.rem(sub + 1, nsub)

    hsend[...] = jnp.zeros_like(hsend)
    for ref in (ph, qh, sh):
        ref[pl.ds(0, VEC), :] = jnp.zeros((VEC, LANES), f32)
    for ref in (yv, kv, xv, rbv, arbv):
        ref[...] = jnp.zeros_like(ref)
    for copy in small:
        copy.wait()
    for q in range(2 * IF):
        for k in range(1, K):
            c = colx[k, sendx[0, q]]
            rimx[k, q] = jnp.where(
                c < IF, c, jnp.where(c < IF + NBLK, 16, c + 8 - IF - NBLK)
            )
    for n in range(NBLK):
        for k in range(1, K):
            c = colx[k, n] - IF
            colx[k, n] = jnp.where((c >= 0) & (c < NBLK), c, NBLK)
    ext[...] = jnp.zeros_like(ext)
    rim[...] = jnp.zeros_like(rim)
    rimg[...] = jnp.zeros_like(rimg)

    def clear(c, _):
        faces[c] = jnp.zeros((K - 1, 16, LANES), f32)
        return 0

    lax.fori_loop(0, CHUNKS, clear, 0)

    lane12 = lax.broadcasted_iota(jnp.int32, (12, LANES), 1)
    row12 = lax.broadcasted_iota(jnp.int32, (12, LANES), 0)
    live = countx[0]
    for c in range(ROWS // LR):
        flat[0, pl.ds(LR * c, LR), :] = rhs_ref[:, pl.ds(c * LANES, LANES)]
        flat[1, pl.ds(LR * c, LR), :] = cot_ref[:, pl.ds(c * LANES, LANES)]
    for r in range(LR):
        chunks = [flat[0, pl.ds(2 * i + r, 12, stride=6), :] for i in range(3)]
        for j, row in enumerate(chunks_to_rows(chunks, lane12)):
            row = jnp.where(row12 * 4 + j < live, row, jnp.zeros_like(row))
            rh[pl.ds(r * NBLK + j, 12, stride=4), :] = row
        chunks = [flat[1, pl.ds(2 * i + r, 12, stride=6), :] for i in range(3)]
        for j, row in enumerate(chunks_to_rows(chunks, lane12)):
            tvec[pl.ds(r * NBLK + j, 12, stride=4), :] = row

    def halves(v):
        hi = v.astype(bf16)
        return hi, (v - hi.astype(f32)).astype(bf16)

    def row_sums(v):
        return [
            jnp.broadcast_to(jnp.sum(p, axis=1, keepdims=True), (8, LANES))
            for p in row_parts(v, lane)
        ]

    def precondition(src, base, dst, dst_base, slot, rd=None):
        full = slot is not None

        def pair(s, _):
            if rd is not None:
                for q in range((nsub - 1) // 3):
                    sum_copy(rd, s * ((nsub - 1) // 3) + q).start()
            tiles = (2 * s, 2 * s + 1)
            at = [pl.multiple_of(8 * t, 8) for t in tiles]
            items = [(b, r) for b in range(2) for r in range(LR)]
            x = {
                (b, r): src[pl.ds(pl.multiple_of(base + r * NBLK + at[b], 8), 8), :]
                for b, r in items
            }
            pat = {m: patterns(x[m], lane) for m in items}
            zero = jnp.zeros((8, LANES), f32)
            proj = {m: zero for m in items}
            acc = {m: [zero] * 3 for m in items}
            for g in range(GROUPS):
                for b in range(2):
                    w = [weights[3 * g + i, pl.ds(at[b], 8), :] for i in range(3)]
                    for r in range(LR):
                        m = (b, r)
                        sums = row_sums([w[i] * pat[m][i] for i in range(3)])
                        for j in range(4):
                            proj[m] = jnp.where(lane == 4 * g + j, sums[j], proj[m])
                        if full:
                            acc[m][0] += w[0] * jnp.where(lane < 96, sums[0], sums[1])
                            acc[m][1] += w[1] * jnp.where(lane < 64, sums[1], sums[2])
                            acc[m][2] += w[2] * jnp.where(lane < 32, sums[2], sums[3])
            for b, r in items:
                dst[pl.ds(pl.multiple_of(dst_base + r * NBLK + at[b], 8), 8), :] = proj[b, r]
                if full:
                    a = acc[b, r]
                    total = (
                        a[0]
                        + pltpu.roll(jnp.where(lane >= 96, a[0], a[1]), 32, 1)
                        + pltpu.roll(jnp.where(lane >= 64, a[1], a[2]), 64, 1)
                        + pltpu.roll(a[2], 96, 1)
                    )
                    ext[slot, pl.ds(pl.multiple_of(r * EXT + at[b], 8), 8), :] = x[
                        b, r
                    ] + jnp.where(lane < 96, total, zero)
            return 0

        lax.fori_loop(0, TILES // 2, pair, 0)

    def halo_copies(h):
        return (
            pltpu.make_async_remote_copy(
                src_ref=hsend.at[h, 0], dst_ref=hrecv.at[h, 1],
                send_sem=hs_sem.at[h, 0], recv_sem=hr_sem.at[h, 1],
                device_id={"sub": before}, device_id_type=MESH,
            ),
            pltpu.make_async_remote_copy(
                src_ref=hsend.at[h, 1], dst_ref=hrecv.at[h, 0],
                send_sem=hs_sem.at[h, 1], recv_sem=hr_sem.at[h, 0],
                device_id={"sub": after}, device_id_type=MESH,
            ),
        )

    def halo_start(h, slot):
        for side in range(2):
            for j in range(IF):
                idx = sendx[0, side * IF + j]
                for r in range(LR):
                    hsend[h, side, pl.ds(r * 8 + j, 1), :] = ext[slot, pl.ds(r * EXT + idx, 1), :]
        for copy in halo_copies(h):
            copy.start()

    def halo_finish(h, dst):
        for copy in halo_copies(h):
            copy.wait_recv()
        for side in range(2):
            edge = jnp.where(sub == (0 if side == 0 else nsub - 1), 0, 1)
            inside = jnp.broadcast_to(edge, (8, LANES)) > 0
            for r in range(LR):
                v = hrecv[h, side, pl.ds(r * 8, 8), :]
                rim[pl.ds(r * RIM + 8 * side, 8), :] = jnp.where(inside, v, jnp.zeros_like(v))
        for q in range(2 * IF):
            for k in range(1, K):
                c = rimx[k, q]
                for r in range(LR):
                    rimg[pl.ds(((k - 1) * LR + r) * 16 + q, 1), :] = rim[pl.ds(r * RIM + c, 1), :]
        out = {}
        for t in range(2):
            pat = [
                [
                    patterns(rimg[pl.ds(((k - 1) * LR + r) * 16 + 8 * t, 8), :], lane)
                    for k in range(1, K)
                ]
                for r in range(LR)
            ]
            acc = [jnp.zeros((8, LANES), f32)] * LR
            for g in range(GROUPS):
                prod = [[None] * 3 for _ in range(LR)]
                for i in range(3):
                    a = [faces[3 * g + i, k, pl.ds(8 * t, 8), :] for k in range(K - 1)]
                    for r in range(LR):
                        prod[r][i] = (a[0] * pat[r][0][i] + a[1] * pat[r][1][i]) + (
                            a[2] * pat[r][2][i]
                        )
                for r in range(LR):
                    for j, v in enumerate(row_sums(prod[r])):
                        acc[r] = jnp.where(lane == 4 * g + j, v, acc[r])
            for r in range(LR):
                out[t, r] = acc[r]
        block = lax.broadcasted_iota(jnp.int32, (NBLK, LANES), 0)
        total = [dst[pl.ds(r * NBLK, NBLK), :] for r in range(LR)]
        for q in range(2 * IF):
            hit = block == sendx[0, q]
            for r in range(LR):
                row = jnp.broadcast_to(out[q // 8, r][q % 8 : q % 8 + 1], (NBLK, LANES))
                total[r] = total[r] + jnp.where(hit, row, jnp.zeros_like(row))
        for r in range(LR):
            dst[pl.ds(r * NBLK, NBLK), :] = total[r]

    def halo_sent(h):
        for copy in halo_copies(h):
            copy.wait_send()

    def stiffness(slot, dst):
        def gather(s, _):
            for q in range(4):
                n = s * 4 + q
                for k in range(1, K):
                    c = colx[k, n]
                    for r in range(LR):
                        gat[pl.ds(((k - 1) * LR + r) * NBLK + n, 1), :] = ext[
                            slot, pl.ds(r * EXT + c, 1), :
                        ]
            return 0

        lax.fori_loop(0, NBLK // 4, gather, 0)

        def tile(t, _):
            at = pl.multiple_of(8 * t, 8)
            pat = []
            for r in range(LR):
                own = ext[slot, pl.ds(pl.multiple_of(r * EXT + 8 * t, 8), 8), :]
                rest = [
                    gat[pl.ds(pl.multiple_of(((k - 1) * LR + r) * NBLK + 8 * t, 8), 8), :]
                    for k in range(1, K)
                ]
                pat.append([patterns(v, lane) for v in [own] + rest])

            out = [jnp.zeros((8, LANES), f32)] * LR
            for g in range(GROUPS):
                prod = [[None] * 3 for _ in range(LR)]
                for i in range(3):
                    a = [blocks[3 * g + i, k, pl.ds(at, 8), :] for k in range(K)]
                    for r in range(LR):
                        prod[r][i] = (a[0] * pat[r][0][i] + a[1] * pat[r][1][i]) + (
                            a[2] * pat[r][2][i] + a[3] * pat[r][3][i]
                        )
                for r in range(LR):
                    for j, v in enumerate(row_sums(prod[r])):
                        out[r] = jnp.where(lane == 4 * g + j, v, out[r])
            for r in range(LR):
                dst[pl.ds(pl.multiple_of(r * NBLK + 8 * t, 8), 8), :] = out[r]
            return 0

        lax.fori_loop(0, TILES, tile, 0)

    def sum_copy(rd, m):
        d = nsub // 2 + lax.div(m + 1, 2) * (2 * lax.rem(m, 2) - 1)
        at = rd * nsub + sub
        return pltpu.make_async_remote_copy(
            src_ref=rbuf.at[at], dst_ref=rbuf.at[at],
            send_sem=rs_sem.at[rd], recv_sem=rr_sem.at[rd],
            device_id={"sub": lax.rem(sub + d, nsub)}, device_id_type=MESH,
        )

    srow = lax.broadcasted_iota(jnp.int32, (8, LANES), 0)

    def sum_local(rd, pairs):
        payload = jnp.zeros((8, LANES), f32)
        for r in range(LR):
            tile = jnp.zeros((8, LANES), f32)
            for d, (a, b) in enumerate(pairs):
                row = jnp.sum(a[r] * b[r], axis=0, keepdims=True)
                tile = jnp.where(srow == d, jnp.broadcast_to(row, (8, LANES)), tile)
            tot = jnp.broadcast_to(jnp.sum(tile, axis=1, keepdims=True), (8, LANES))
            payload = jnp.where(lane == srow + 64 * r, tot, payload)
        rbuf[rd * nsub + sub] = jnp.sum(payload, axis=0, keepdims=True)

    def sum_finish(rd):
        span = rbuf.at[pl.ds(rd * nsub, nsub - 1)]
        pltpu.make_async_copy(span, span, rr_sem.at[rd]).wait()
        parts = [jnp.zeros((1, LANES), f32)] * 4
        for s in range(nsub):
            parts[s % 4] = parts[s % 4] + rbuf[rd * nsub + s]
        row = jnp.broadcast_to((parts[0] + parts[1]) + (parts[2] + parts[3]), (8, LANES))
        pltpu.make_async_copy(span, span, rs_sem.at[rd]).wait()
        return [
            jnp.broadcast_to(
                jnp.sum(
                    jnp.where(lane == srow + 64 * r, row, jnp.zeros_like(row)),
                    axis=1, keepdims=True,
                ),
                (8, LANES),
            )
            for r in range(LR)
        ]

    def factor_row(src, j, kind):
        return pl.multiple_of(((src * ITERS + j) * 2 + kind) * VEC, 8)

    def factor_copy(buf, left, j, kind, d, src, target):
        at = factor_row(src, j, kind)
        piece = (j * 2 + left) * 2 + kind
        return pltpu.make_async_remote_copy(
            src_ref=buf.at[pl.ds(at, VEC), :], dst_ref=buf.at[pl.ds(at, VEC), :],
            send_sem=fs_sem.at[piece * 4 + d], recv_sem=fr_sem.at[piece * 4 + src],
            device_id={"rhs": target}, device_id_type=MESH,
        )

    def factor_send(buf, left, j, kind):
        for d in range(1, nrhs):
            factor_copy(buf, left, j, kind, d, me, lax.rem(me + d, nrhs)).start()

    def weight_copy(it, d, src, target):
        at = src * 2 + it
        return pltpu.make_async_remote_copy(
            src_ref=nf.at[at], dst_ref=nf.at[at],
            send_sem=ns_sem.at[it * 4 + d], recv_sem=nr_sem.at[at],
            device_id={"rhs": target}, device_id_type=MESH,
        )

    def rows(ref, i):
        return [
            ref[pl.ds(pl.multiple_of(i * VEC + r * NBLK, 8), NBLK), :] for r in range(LR)
        ]

    def put(ref, i, v):
        for r in range(LR):
            ref[pl.ds(pl.multiple_of(i * VEC + r * NBLK, 8), NBLK), :] = v[r]

    def put_at(ref, base, v):
        for r in range(LR):
            ref[pl.ds(pl.multiple_of(base + r * NBLK, 8), NBLK), :] = v[r]

    def ext_rows(slot):
        return [ext[slot, pl.ds(r * EXT, NBLK), :] for r in range(LR)]

    def axpy(x, s, y):
        return [a + c * b for a, c, b in zip(x, s, y)]

    def scale(s, y):
        return [c * b for c, b in zip(s, y)]

    def keep(kind, i, v):
        for r in range(LR):
            scr[pl.ds((r * 6 + kind) * ITERS + i, 1), :] = v[r]

    def kept(kind, i):
        return [scr[pl.ds((r * 6 + kind) * ITERS + i, 1), :] for r in range(LR)]

    for copy in pre_copies:
        copy.wait()
    precondition(rh, 0, uh, 0, 0)
    pl.semaphore_wait(barrier, peers)
    halo_start(0, 0)
    put(zh, 0, ext_rows(0))
    precondition(tvec, 0, utv, 0, 1)
    halo_start(1, 1)
    put(tmv, 0, ext_rows(1))
    for n in range(NBLK):
        stiff_copy(n).wait()

    def face(c, _):
        for k in range(1, K):
            for q in range(2 * IF):
                faces[c, k - 1, pl.ds(q, 1), :] = blocks[c, k, pl.ds(sendx[0, q], 1), :]
        return 0

    lax.fori_loop(0, CHUNKS, face, 0)
    stiffness(0, nvec)
    halo_finish(0, nvec)
    put(wh, 0, rows(nvec, 0))
    stiffness(1, atv)
    halo_finish(1, atv)
    halo_sent(0)
    halo_sent(1)

    def forward(i, carry):
        rho_old, gamma_old, c_old = carry[:3]
        z, w, res, t = rows(zh, i), rows(wh, i), rows(rh, i), rows(tvec, 0)
        q_old, s_old = rows(qh, i), rows(sh, i)
        sum_local(
            i,
            (
                (res, z), (z, w), (z, q_old), (t, z),
                (t, s_old), (w, s_old), (q_old, s_old),
            ),
        )
        precondition(wh, i * VEC, hvec, 0, 0, i)
        halo_start(2 + i, 0)
        at = factor_row(me, i, 0)
        put_at(fl, at, rows(uh, i))
        at = factor_row(me, i, 1)
        put_at(fr, at, rows(rh, i))
        factor_send(fl, 1, i, 0)
        factor_send(fr, 0, i, 1)
        stiffness(0, nvec)
        halo_finish(2 + i, nvec)
        halo_sent(2 + i)
        tot = sum_finish(i)
        val = [[tot[r][d : d + 1, :] for r in range(LR)] for d in range(7)]
        rho, za, zq, tz = val[:4]
        first = jnp.broadcast_to(jnp.where(i == 0, 1, 0), (1, LANES)) > 0
        beta = [jnp.where(first, 0.0, a / b) for a, b in zip(rho, rho_old)]
        gamma = [
            za[r] + beta[r] * (2.0 * zq[r] + beta[r] * gamma_old[r]) for r in range(LR)
        ]
        c = axpy(tz, beta, c_old)
        alpha = [a / b for a, b in zip(rho, gamma)]
        minus = [-a for a in alpha]
        for kind, v in enumerate((alpha, gamma, rho, beta, c, zq)):
            keep(kind, i, v)
        p = axpy(rows(zh, i), beta, rows(ph, i))
        put(ph, i + 1, p)
        put(xv, 0, axpy(rows(xv, 0), alpha, p))
        q = axpy(rows(wh, i), beta, rows(qh, i))
        put(qh, i + 1, q)
        put(rh, i + 1, axpy(rows(rh, i), minus, q))
        s = axpy(ext_rows(0), beta, rows(sh, i))
        put(sh, i + 1, s)
        put(zh, i + 1, axpy(rows(zh, i), minus, s))
        y = axpy(rows(nvec, 0), beta, rows(yv, 0))
        put(yv, 0, y)
        put(wh, i + 1, axpy(rows(wh, i), minus, y))
        k = axpy(rows(hvec, 0), beta, rows(kv, 0))
        put(kv, 0, k)
        put(uh, i + 1, axpy(rows(uh, i), minus, k))
        return (
            tuple(rho), tuple(gamma), tuple(c),
            tuple(val[4]), tuple(val[5]), tuple(val[6]),
        )

    none = (jnp.zeros((1, LANES), jnp.float32),) * LR
    one = (jnp.ones((1, LANES), jnp.float32),) * LR
    last = lax.fori_loop(0, ITERS, forward, (one, none, none, none, none, none))
    gamma3, c3, ts, ws, qs = last[1:]

    def adjoint(i, bb, e0, e1, norm_bar, pb, wp, mp, amp, it=None):
        ratio = [a / b for a, b in zip(bb, kept(2, i))]
        full = [a + b for a, b in zip(norm_bar, ratio)]
        twice = [2.0 * a for a in full]
        zq, beta = kept(5, i + 1), kept(3, i + 1)
        err = [e0[r] + twice[r] * zq[r] + e1[r] for r in range(LR)]
        if it is None:
            put_at(fr, factor_row(me, i + 1, 0), axpy(pb, full, rows(rh, i + 1)))
            put_at(fl, factor_row(me, i + 1, 1), axpy(wp, full, rows(uh, i + 1)))
            factor_send(fr, 0, i + 1, 0)
            factor_send(fl, 1, i + 1, 1)
        else:
            tile = [jnp.broadcast_to(a, (8, LANES)) for a in full]
            nf[me * 2 + it] = jnp.where(srow == 0, tile[0], tile[1])
            for d in range(1, nrhs):
                weight_copy(it, d, me, lax.rem(me + d, nrhs)).start()
        rb = axpy([a + b for a, b in zip(rows(rbv, 0), mp)], twice, rows(zh, i + 1))
        put(rbv, 0, rb)
        arb = axpy([a + b for a, b in zip(rows(arbv, 0), amp)], twice, rows(wh, i + 1))
        put(arbv, 0, arb)
        alpha, gamma = kept(0, i), kept(1, i)
        step_bar = [a - b for a, b in zip(kept(4, i), err)]
        curv2 = [-2.0 * (s * a / g) for s, a, g in zip(step_bar, alpha, gamma)]
        norm_bar = [s / g - a * b for s, g, a, b in zip(step_bar, gamma, ratio, beta)]
        diff = [a - b for a, b in zip(rows(tvec, 0), arb)]
        pb = axpy(axpy(scale(beta, pb), alpha, diff), curv2, rows(qh, i + 1))
        put(pbv, 0, pb)
        return tuple(norm_bar)

    alpha3, beta3, zq3 = kept(0, 3), kept(3, 3), kept(5, 3)
    gamma2, c2 = kept(1, 2), kept(4, 2)
    g2 = [-2.0 * (c * a / g) for c, a, g in zip(c3, alpha3, gamma3)]
    mix = lambda a, b: axpy(scale(alpha3, a), g2, b)
    bb = [
        alpha3[r] * c2[r] + g2[r] * (zq3[r] + beta3[r] * gamma2[r]) for r in range(LR)
    ]
    e1 = [alpha3[r] * ts[r] + g2[r] * (ws[r] + beta3[r] * qs[r]) for r in range(LR)]
    norm_bar = adjoint(
        2, bb, none, e1, [c / g for c, g in zip(c3, gamma3)],
        mix(rows(tvec, 0), rows(qh, 4)),
        mix(rows(utv, 0), rows(kv, 0)),
        mix(rows(tmv, 0), rows(sh, 4)),
        mix(rows(atv, 0), rows(yv, 0)),
    )

    def backward(it, norm_bar):
        i = 1 - it
        rd = ITERS + it
        pb = rows(pbv, 0)
        sum_local(
            rd,
            (
                (pb, rows(ph, i + 1)),
                (rows(rbv, 0), rows(qh, i + 1)),
                (pb, rows(sh, i + 1)),
            ),
        )
        precondition(pbv, 0, hvec, 0, 0, rd)
        halo_start(2 + rd, 0)
        put_at(fr, factor_row(me, i + 1, 0), rows(pbv, 0))
        factor_send(fr, 0, i + 1, 0)
        put_at(fl, factor_row(me, i + 1, 1), rows(hvec, 0))
        factor_send(fl, 1, i + 1, 1)
        stiffness(0, nvec)
        halo_finish(2 + rd, nvec)
        halo_sent(2 + rd)
        tot = sum_finish(rd)
        bb, e0, e1 = [[tot[r][d : d + 1, :] for r in range(LR)] for d in range(3)]
        return adjoint(
            i, bb, e0, e1, norm_bar,
            rows(pbv, 0), rows(hvec, 0), ext_rows(0), rows(nvec, 0), it,
        )

    norm_bar = lax.fori_loop(0, 2, backward, norm_bar)

    zeta = factor_row(me, 0, 0)
    put_at(fr, zeta, axpy(rows(pbv, 0), norm_bar, rows(rh, 0)))
    factor_send(fr, 0, 0, 0)
    precondition(fr, zeta, fl, factor_row(me, 0, 1), None)
    factor_send(fl, 1, 0, 1)

    for r in range(LR):
        parts = [xv[pl.ds(r * NBLK + j, 12, stride=4), :] for j in range(4)]
        for i, chunk in enumerate(rows_to_chunks(parts, lane12)):
            flat[0, pl.ds(2 * i + r, 12, stride=6), :] = chunk
    for c in range(ROWS // LR):
        sol_ref[:, pl.ds(c * LANES, LANES)] = flat[0, pl.ds(LR * c, LR), :]

    def factors_wait(j, _):
        for left, buf in ((1, fl), (0, fr)):
            for kind in range(2):
                for d in range(1, nrhs):
                    src = lax.rem(me + d, nrhs)
                    factor_copy(buf, left, j, kind, d, src, src).wait_recv()
                    factor_copy(buf, left, j, kind, d, me, src).wait_send()
        return 0

    lax.fori_loop(0, ITERS, factors_wait, 0)
    for it in range(2):
        for d in range(1, nrhs):
            src = lax.rem(me + d, nrhs)
            weight_copy(it, d, src, src).wait_recv()
            weight_copy(it, d, me, src).wait_send()

    def finish(src, _):
        for it in range(2):
            j = 2 - it
            weight = nf[src * 2 + it]
            for buf, kind in ((fr, 0), (fl, 1)):
                at, other = factor_row(src, j, kind), factor_row(src, j, 1 - kind)
                for r in range(LR):
                    here = pl.ds(pl.multiple_of(at + r * NBLK, 8), NBLK)
                    there = pl.ds(pl.multiple_of(other + r * NBLK, 8), NBLK)
                    buf[here, :] = buf[here, :] + weight[r : r + 1] * buf[there, :]
        return 0

    lax.fori_loop(0, nrhs, finish, 0)

    depth = nrhs * ITERS * 2 * LR
    lane24 = lax.broadcasted_iota(jnp.int32, (24, LANES), 1)

    def grads(t, _):
        for s in range(8):
            n = t * 8 + s
            lh, ll = halves(fl[pl.ds(n, depth, stride=NBLK), :])
            rhi, rlo = halves(fr[pl.ds(n, depth, stride=NBLK), :])
            gb[s] = lax.dot_general(
                jnp.concatenate([lh, lh, ll], axis=0),
                jnp.concatenate([rhi, rlo, rhi], axis=0),
                (((0,), (0,)), ((), ())),
                preferred_element_type=jnp.float32,
            )
            parts = [gb[s, pl.ds(j, 24, stride=4), :] for j in range(4)]
            for i, chunk in enumerate(rows_to_chunks(parts, lane24)):
                go[pl.ds(t * (CHUNKS * 8) + i * 8 + s, 24, stride=24), :] = chunk
        return 0

    lax.fori_loop(0, TILES, grads, 0)


def shards(nsub, nrhs, stiffness, precond, rhs_vec, cotangent, col_index, send_rows, counts):
    stiff = stiffness.reshape(NBLK, K, CHUNKS, LANES).transpose(0, 2, 1, 3)
    pre = precond.reshape(TILES, 8, CHUNKS, LANES).transpose(0, 2, 1, 3)
    f32 = jnp.float32
    vmem = pl.BlockSpec(memory_space=pltpu.VMEM)
    hbm = pl.BlockSpec(memory_space=pltpu.HBM)

    def vec(count=1):
        return pltpu.VMEM((count * VEC, LANES), f32)

    dma = pltpu.SemaphoreType.DMA
    factors = nrhs * ITERS * 2 * VEC
    sol, grad = pl.pallas_call(
        functools.partial(kernel, nsub, nrhs),
        out_shape=(
            jax.ShapeDtypeStruct((LR, NBLK * BS), f32),
            jax.ShapeDtypeStruct((TILES * CHUNKS * 8, LANES), f32),
        ),
        in_specs=[hbm, hbm, hbm, vmem, vmem, hbm, hbm],
        out_specs=(vmem, vmem),
        scratch_shapes=[
            pltpu.SMEM((K, NBLK), jnp.int32),
            pltpu.SMEM((K, 2 * IF), jnp.int32),
            pltpu.SMEM((1, 2 * IF), jnp.int32),
            pltpu.SMEM((1,), jnp.int32),
            pltpu.VMEM((2, ROWS, LANES), f32),
            pltpu.VMEM((CHUNKS, K, NBLK, LANES), f32),
            pltpu.VMEM((CHUNKS, K - 1, 16, LANES), f32),
            pltpu.VMEM((CHUNKS, NBLK, LANES), f32),
            pltpu.VMEM((2, LR * EXT, LANES), f32),
            vec(K - 1),
            pltpu.VMEM((LR * RIM, LANES), f32),
            pltpu.VMEM(((K - 1) * LR * 16, LANES), f32),
        ]
        + [vec() for _ in range(12)]
        + [vec(ITERS + 1) for _ in range(7)]
        + [
            pltpu.VMEM((LR * 6 * ITERS, LANES), f32),
            pltpu.VMEM((HALOS, 2, LR * 8, LANES), f32),
            pltpu.VMEM((HALOS, 2, LR * 8, LANES), f32),
            pltpu.VMEM((REDS * nsub, 1, LANES), f32),
            pltpu.VMEM((factors, LANES), f32),
            pltpu.VMEM((factors, LANES), f32),
            pltpu.VMEM((nrhs * 2, 8, LANES), f32),
            pltpu.VMEM((8, LANES, LANES), f32),
            dma((NBLK + TILES,)),
            dma((3,)),
            dma((HALOS, 2)),
            dma((HALOS, 2)),
            dma((REDS,)),
            dma((REDS,)),
            dma((ITERS * 16,)),
            dma((ITERS * 16,)),
            dma((8,)),
            dma((nrhs * 2,)),
        ],
        compiler_params=pltpu.CompilerParams(
            collective_id=0, has_side_effects=True, vmem_limit_bytes=62 * 1024 * 1024
        ),
        name="cg_adjoint",
    )(col_index.T, send_rows, counts, rhs_vec, cotangent, stiff, pre)
    grad = grad.reshape(TILES, CHUNKS, 8, LANES).transpose(0, 2, 1, 3)
    return sol, grad.reshape(NBLK, BS * BS)


def solution(mesh):
    in_specs = (
        P("sub", None, None),
        P("sub", None),
        P("rhs", "sub"),
        P("rhs", "sub"),
        P("sub", None),
        P("sub", None),
        P("sub"),
    )
    out_specs = (P("rhs", "sub"), P("sub", None))
    body = functools.partial(shards, mesh.shape["sub"], mesh.shape["rhs"])
    return jax.shard_map(body, mesh=mesh, in_specs=in_specs, out_specs=out_specs, check_vma=False)
```
